128 devices in a mesh: row: 8 (over z, x_hi), col: 16 (over y, x_lo, core).
Axes of the slice: x: 4 (x_hi: 2, x_lo: 2; x = x_hi * 2 + x_lo), y: 4, z: 4, core: 2. Of those that a mesh axis runs over, the one named last changes fastest.
Arguments:
- panels: bfloat16 [8, 16, 512, 1024], P('row', 'col'), may hold values from -1 to 1
- stacks: int32 [3, 8, 16, 16, 512], P(None, 'row', 'col'), may hold values from 0 to 512, as said below
Outputs:
- product: float32 [8, 16, 512, 1024], P('row', 'col')
The draws below stay inside these ranges and needn't reach their ends.
Inputs may be any that keep to these rules, and one draw needn't show every extreme that they name: `stacks`: component 0 and 1 of every entry index tiles of a panel and component 2 a tile of the product or 512. In each list of one grid cell and shift the live entries (target below 512) come first and the rest have target 512; all lists of one grid cell hold the same number of live entries, which differs between grid cells; some grid cell has only live entries and some has padding.
All inputs are finite; a program needn't handle non-finite values.
Results may differ from the reference program's by a relative error of at most 0.0003.
Values may be sent and summed in bfloat16 or wider, within the bound.
A program may use at most 128 MiB of HBM per device.

```python
import jax
import jax.numpy as jnp
from jax import lax

TB = 32
TPD = 512
STK = 512
N_ROW = 8
N_COL = 16


def draw_stacks(key, part):
    keys = jax.random.split(jax.random.fold_in(key, 7), 4)
    divisor = jax.random.randint(keys[0], (N_ROW, N_COL), 1, 8)
    divisor = divisor.at[0, 0].set(1).at[0, 1].set(4)
    live_count = STK // divisor
    shape = (N_ROW, N_COL, N_COL, STK)
    left_index = jax.random.randint(keys[1], shape, 0, TPD)
    right_index = jax.random.randint(keys[2], shape, 0, TPD)
    target = jax.random.randint(keys[3], shape, 0, TPD)
    position = lax.broadcasted_iota(jnp.int32, shape, 3)
    target = jnp.where(position < live_count[:, :, None, None], target, TPD)
    return jnp.stack([left_index, right_index, target]).astype(jnp.int32)


def level_of(own_key, extent, cuts, low, top_value):
    loudness, own = 1.0, jax.random.fold_in(own_key, 6)
    for dim, shards_of in cuts:
        draws = jnp.exp(jax.random.uniform(jax.random.fold_in(own, dim), (shards_of,), jnp.float32, low / len(cuts), top_value / len(cuts)))
        loudness = loudness * jnp.repeat(draws, extent[dim] // shards_of).reshape([-1 if axis == dim else 1 for axis in range(len(extent))])
    return loudness


def scatter_about(key, dims, spread, reach, cuts=(), kind=jnp.bfloat16):
    values = spread * jax.random.normal(key, dims, jnp.float32)
    if cuts:
        values = values * level_of(key, dims, cuts, -0.22, 0.18)
    return jnp.clip(values, -reach, reach).astype(kind)


def setup_inputs(seed: int = 0) -> dict:
    streams_of = jax.random.split(jax.random.key(seed), 3)
    panels = scatter_about(streams_of[0], (N_ROW, N_COL, TPD, TB * TB), 0.18, 1.0, ((0, 8), (1, 16)))
    stacks = draw_stacks(jax.random.fold_in(streams_of[2], 71), 0)
    return {"panels": panels, "stacks": stacks}


def reference(panels, stacks):
    images_per_row = N_COL // N_ROW
    tile_grid = panels.astype(jnp.float32).reshape(N_ROW, N_COL, TPD, TB, TB)
    shift_grid = jnp.broadcast_to(jnp.arange(N_COL, dtype=jnp.int32)[:, None], (N_COL, STK))

    def one_cell(flat_index):
        row_index = flat_index // N_COL
        col_index = flat_index % N_COL
        by_row = lax.dynamic_index_in_dim(stacks, row_index, 1, keepdims=False)
        stack_lists = lax.dynamic_index_in_dim(by_row, col_index, 1, keepdims=False)
        left_panels = lax.dynamic_index_in_dim(tile_grid, row_index, 0, keepdims=False)
        right_panels = lax.dynamic_index_in_dim(tile_grid, col_index, 1, keepdims=False)
        left_rows = left_panels[shift_grid, stack_lists[0]]
        right_rows = right_panels[shift_grid // images_per_row, stack_lists[1]]
        product = jnp.einsum("gsij,gsjk->gsik", left_rows, right_rows)
        totals = jnp.zeros((TPD + 1, TB, TB), jnp.float32)
        totals = totals.at[stack_lists[2].reshape(-1)].add(product.reshape(-1, TB, TB))
        return totals[:TPD].reshape(TPD, TB * TB)

    result = lax.map(one_cell, jnp.arange(N_ROW * N_COL, dtype=jnp.int32))
    return result.reshape(N_ROW, N_COL, TPD, TB * TB)
```

```python
import functools
import jax
import jax.numpy as jnp
from jax import lax
from jax.experimental import pallas as pl
from jax.sharding import PartitionSpec as P_
from jax.experimental.pallas import tpu as pltpu
TPD=512; STK=512
ROWS=520
PAD=64
def make(H=8, UG=8, flags=None):
    def kernel(a_s,b_s,t_s,st,L,R,out,C0,C1,C2,C3,P):
        C=[C0,C1,C2,C3]
        h=pl.program_id(0)
        lg=lax.broadcasted_iota(jnp.int32,(32,128),1)//32
        keep=[lg==s for s in range(4)]
        lt2=lg<2
        zero=jnp.zeros((32,128),jnp.bfloat16)
        @pl.when(h==0)
        def _():
            P[...]=jnp.zeros(P.shape,jnp.float32)
            def z(i,_):
                for s in range(4):
                    C[s][pl.ds(pl.multiple_of(i*2,2),2)]=jnp.zeros((2,32,128),jnp.float32)
                return 0
            lax.fori_loop(0,ROWS//2,z,0)
        for d in range(4):
            s_=[st[h*32+d*4+p] for p in range(4)]
            e_=[st[h*32+d*4+p+1] for p in range(4)]
            n=functools.reduce(jnp.maximum,[e-s for s,e in zip(s_,e_)])
            nb=(n+UG-1)//UG
            off=h*1024+PAD
            def body(i,_,s_=s_,e_=e_,d=d):
                base=[s+off+i*UG for s in s_]
                end=[jnp.where(i>0,e+off,0) for e in e_]
                for u in range(UG):
                    v=P[u]
                    for p in range(4):
                        ix=base[p]+(u-UG)
                        t=jnp.where(ix<end[p],t_s[ix],TPD)
                        c=C[(p+d)%4]
                        c[t]=c[t]+v
                for u in range(UG):
                    av=[];bv=[]
                    for p in range(4):
                        ix=base[p]+u
                        av.append(L[a_s[ix]]); bv.append(R[b_s[ix]])
                    lhs=jnp.where(lt2,jnp.where(keep[0],av[0],av[1]),jnp.where(keep[2],av[2],av[3]))
                    rhs=jnp.concatenate([jnp.where(keep[(p+d)%4],bv[p],zero) for p in range(4)],axis=0)
                    P[u]=jnp.dot(lhs,rhs,preferred_element_type=jnp.float32)
                return 0
            lax.fori_loop(0,jnp.where(n>0,nb+1,0),body,0)
        @pl.when(h==H-1)
        def _():
            lgb=lax.broadcasted_iota(jnp.int32,(32,128),1)//32
            n2=lgb<2; n1=(lgb%2)==0
            def fin(i,_):
                rows=pl.ds(pl.multiple_of(i*32,32),32)
                for c in range(8):
                    w=[]
                    for k in range(4):
                        x=[C[s][rows,4*c+k,:] for s in range(4)]
                        w.append(jnp.where(n2,jnp.where(n1,x[0],x[1]),jnp.where(n1,x[2],x[3])))
                    z=[jnp.where(n2,w[k],w[k+2])+pltpu.roll(jnp.where(n2,w[k+2],w[k]),64,1) for k in range(2)]
                    y=jnp.where(n1,z[0],z[1])
                    o=jnp.where(n1,z[1],z[0])
                    sw=jnp.where(n1,pltpu.roll(o,96,1),pltpu.roll(o,32,1))
                    out[rows,c*128:(c+1)*128]=y+sw
                return 0
            lax.fori_loop(0,TPD//32,fin,0)
    return pl.pallas_call(kernel,
        out_shape=jax.ShapeDtypeStruct((TPD,1024),jnp.float32),
        grid_spec=pltpu.PrefetchScalarGridSpec(num_scalar_prefetch=4,grid=(H,),
            in_specs=[pl.BlockSpec((256,32,128),lambda h,*_:(h,0,0)),
                      pl.BlockSpec((128,32,128),lambda h,*_:(h,0,0))],
            out_specs=pl.BlockSpec((TPD,1024),lambda h,*_:(0,0)),
            scratch_shapes=[pltpu.VMEM((ROWS,32,128),jnp.float32)]*4+[pltpu.VMEM((UG,32,128),jnp.float32)]),
        compiler_params=pltpu.CompilerParams(vmem_limit_bytes=62*2**20,dimension_semantics=("arbitrary",),flags=flags or {}))
def pack(x):
    s=x.shape[:-2]; n=len(s)
    return jnp.moveaxis(x.reshape(s+(128,4,32,32)),n+1,n+2).reshape(s+(128,32,128))
def prep(stacks):
    a,b,t=stacks[0],stacks[1],stacks[2]
    G=a.shape[0]
    g=lax.broadcasted_iota(jnp.int32,a.shape,0)
    cls=jnp.where(t<TPD,((b-a)&3)*4+(a&3),16)
    ap=a+(g&1)*TPD
    key=(cls<<25)|((ap>>2)<<17)|((b>>2)<<10)|t
    key=key.reshape(G//2,2*STK)
    cl=cls.reshape(G//2,2*STK)
    st=jnp.sum((cl[:,:,None]<lax.broadcasted_iota(jnp.int32,(1,1,32),2)).astype(jnp.int32),axis=1)
    k=lax.sort(key,dimension=1,is_stable=False).reshape(-1)
    k=jnp.pad(k,(PAD,PAD))
    return (k>>17)&255,(k>>10)&127,k&1023,st.reshape(-1)


def local(panels, stacks):
    own = pack(panels[0, 0])
    right = lax.all_gather(own, "row", axis=0, tiled=True)
    left = lax.all_gather(own, "col", axis=0, tiled=True)
    index = prep(stacks[:, 0, 0])
    out = make(8, 8)(*index, left, right)
    return out.reshape(1, 1, TPD, 1024)


def solution(mesh):
    in_specs = (P_("row", "col", None, None), P_(None, "row", "col", None, None))
    out_specs = P_("row", "col", None, None)
    return jax.shard_map(local, mesh=mesh, in_specs=in_specs, out_specs=out_specs, check_vma=False)
```

```python
import functools
import jax
import jax.numpy as jnp
from jax import lax
from jax.experimental import pallas as pl
from jax.sharding import PartitionSpec as P_
from jax.experimental.pallas import tpu as pltpu
TPD=512; STK=512
ROWS=520
PAD=64
def make(H=8, UG=8, flags=None):
    def kernel(a_s,b_s,t_s,st,L,R,out,C0,C1,C2,C3,P):
        C=[C0,C1,C2,C3]
        h=pl.program_id(0)
        lg=lax.broadcasted_iota(jnp.int32,(32,128),1)//32
        keep=[lg==s for s in range(4)]
        lt2=lg<2
        zero=jnp.zeros((32,128),jnp.bfloat16)
        @pl.when(h==0)
        def _():
            P[...]=jnp.zeros(P.shape,jnp.float32)
            def z(i,_):
                for s in range(4):
                    C[s][pl.ds(pl.multiple_of(i*64,64),64),:]=jnp.zeros((64,128),jnp.float32)
                return 0
            lax.fori_loop(0,ROWS//2,z,0)
        for d in range(4):
            s_=[st[h*32+d*4+p] for p in range(4)]
            e_=[st[h*32+d*4+p+1] for p in range(4)]
            n=functools.reduce(jnp.maximum,[e-s for s,e in zip(s_,e_)])
            nb=(n+UG-1)//UG
            off=h*1024+PAD
            def body(i,_,s_=s_,e_=e_,d=d):
                base=[s+off+i*UG for s in s_]
                end=[jnp.where(i>0,e+off,0) for e in e_]
                for u in range(UG):
                    v=P[u]
                    for p in range(4):
                        ix=base[p]+(u-UG)
                        t=jnp.where(ix<end[p],t_s[ix],TPD)
                        c=C[(p+d)%4]
                        w_=pl.ds(pl.multiple_of(t*32,32),32); c[w_,:]=c[w_,:]+v
                for u in range(UG):
                    av=[];bv=[]
                    for p in range(4):
                        ix=base[p]+u
                        av.append(L[a_s[ix]]); bv.append(R[b_s[ix]])
                    lhs=jnp.where(lt2,jnp.where(keep[0],av[0],av[1]),jnp.where(keep[2],av[2],av[3]))
                    rhs=jnp.concatenate([jnp.where(keep[(p+d)%4],bv[p],zero) for p in range(4)],axis=0)
                    P[u]=jnp.dot(lhs,rhs,preferred_element_type=jnp.float32)
                return 0
            lax.fori_loop(0,jnp.where(n>0,nb+1,0),body,0)
        @pl.when(h==H-1)
        def _():
            lgb=lax.broadcasted_iota(jnp.int32,(32,128),1)//32
            n2=lgb<2; n1=(lgb%2)==0
            def fin(i,_):
                rows=pl.ds(pl.multiple_of(i*32,32),32)
                for c in range(8):
                    w=[]
                    for k in range(4):
                        x=[C[s][pl.ds(i*1024+(4*c+k),32,stride=32),:] for s in range(4)]
                        w.append(jnp.where(n2,jnp.where(n1,x[0],x[1]),jnp.where(n1,x[2],x[3])))
                    z=[jnp.where(n2,w[k],w[k+2])+pltpu.roll(jnp.where(n2,w[k+2],w[k]),64,1) for k in range(2)]
                    y=jnp.where(n1,z[0],z[1])
                    o=jnp.where(n1,z[1],z[0])
                    sw=jnp.where(n1,pltpu.roll(o,96,1),pltpu.roll(o,32,1))
                    out[rows,c*128:(c+1)*128]=y+sw
                return 0
            lax.fori_loop(0,TPD//32,fin,0)
    return pl.pallas_call(kernel,
        out_shape=jax.ShapeDtypeStruct((TPD,1024),jnp.float32),
        grid_spec=pltpu.PrefetchScalarGridSpec(num_scalar_prefetch=4,grid=(H,),
            in_specs=[pl.BlockSpec((256,32,128),lambda h,*_:(h,0,0)),
                      pl.BlockSpec((128,32,128),lambda h,*_:(h,0,0))],
            out_specs=pl.BlockSpec((TPD,1024),lambda h,*_:(0,0)),
            scratch_shapes=[pltpu.VMEM((ROWS*32,128),jnp.float32)]*4+[pltpu.VMEM((UG,32,128),jnp.float32)]),
        compiler_params=pltpu.CompilerParams(vmem_limit_bytes=62*2**20,dimension_semantics=("arbitrary",),flags=flags or {}))
def pack(x):
    s=x.shape[:-2]; n=len(s)
    return jnp.moveaxis(x.reshape(s+(128,4,32,32)),n+1,n+2).reshape(s+(128,32,128))
def prep(stacks):
    a,b,t=stacks[0],stacks[1],stacks[2]
    G=a.shape[0]
    g=lax.broadcasted_iota(jnp.int32,a.shape,0)
    cls=jnp.where(t<TPD,((b-a)&3)*4+(a&3),16)
    ap=a+(g&1)*TPD
    key=(cls<<25)|((ap>>2)<<17)|((b>>2)<<10)|t
    key=key.reshape(G//2,2*STK)
    cl=cls.reshape(G//2,2*STK)
    st=jnp.sum((cl[:,:,None]<lax.broadcasted_iota(jnp.int32,(1,1,32),2)).astype(jnp.int32),axis=1)
    k=lax.sort(key,dimension=1,is_stable=False).reshape(-1)
    k=jnp.pad(k,(PAD,PAD))
    return (k>>17)&255,(k>>10)&127,k&1023,st.reshape(-1)

def pack_kernel(x, o, xf, of):
    lgq = lax.broadcasted_iota(jnp.int32, (128, 128), 1) // 32
    n2 = lgq < 2
    n1 = (lgq % 2) == 0

    def swap(x, y, sh, mask):
        return jnp.where(mask, x, pltpu.roll(y, sh, 1)), jnp.where(mask, pltpu.roll(x, 128 - sh, 1), y)

    for c in range(8):
        xf[...] = x[:, c * 128:(c + 1) * 128].astype(jnp.float32)
        v = [xf[pl.ds(q, 128, stride=4), :] for q in range(4)]
        v[0], v[2] = swap(v[0], v[2], 64, n2)
        v[1], v[3] = swap(v[1], v[3], 64, n2)
        v[0], v[1] = swap(v[0], v[1], 32, n1)
        v[2], v[3] = swap(v[2], v[3], 32, n1)
        for w in range(4):
            of[pl.ds(4 * c + w, 128, stride=32), :] = v[w]

    def cast(i, _):
        rows = pl.ds(pl.multiple_of(i * 512, 512), 512)
        o[rows, :] = of[rows, :].astype(jnp.bfloat16)
        return 0

    lax.fori_loop(0, 8, cast, 0)


def pack_tiles(x):
    return pl.pallas_call(
        pack_kernel,
        out_shape=jax.ShapeDtypeStruct((4096, 128), jnp.bfloat16),
        in_specs=[pl.BlockSpec(memory_space=pltpu.VMEM)],
        out_specs=pl.BlockSpec(memory_space=pltpu.VMEM),
        scratch_shapes=[pltpu.VMEM((512, 128), jnp.float32), pltpu.VMEM((4096, 128), jnp.float32)],
    )(x).reshape(128, 32, 128)
NC = 4


def gather_kernel(own, left, right, local_sem, send, recv):
    r = lax.axis_index("row"); c = lax.axis_index("col")
    xl = lax.rem(c // 2, 2); k = lax.rem(c, 2); xh = lax.rem(r, 2)
    yp, ym = lax.rem(c + 4, 16), lax.rem(c + 12, 16)
    cx, ck = c + 2 - 4 * xl, c + 1 - 2 * k
    cxp, cxm = lax.rem(cx + 4, 16), lax.rem(cx + 12, 16)
    zp, zm = lax.rem(r + 2, 8), lax.rem(r + 6, 8)
    rx = r + 1 - 2 * xh
    rxp, rxm = lax.rem(rx + 2, 8), lax.rem(rx + 6, 8)
    y2, yx2 = lax.rem(c + 8, 16), lax.rem(cx + 8, 16)
    barrier = pltpu.get_barrier_semaphore()
    for d in ((r, yp), (r, ym), (r, cx), (r, ck), (zp, c), (zm, c), (rx, cx)):
        pl.semaphore_signal(barrier, inc=1, device_id=d, device_id_type=pl.DeviceIdType.MESH)
    pl.semaphore_wait(barrier, 7)
    copies = {}
    rows = own.shape[0] // NC

    def go(name, src, dst, device, j):
        n = len(copies)
        piece = pl.ds(j * rows, rows)
        cp = pltpu.make_async_remote_copy(src_ref=src.at[piece], dst_ref=dst.at[piece], send_sem=send.at[n],
                                          recv_sem=recv.at[n], device_id=device, device_id_type=pl.DeviceIdType.MESH)
        cp.start()
        copies[name, j] = cp

    def lf(name, i, device, j):
        go(name, left.at[i], left.at[i], device, j)

    def rt(name, i, device, j):
        go(name, right.at[i], right.at[i], device, j)

    def got(name, j):
        copies[name, j].wait_recv()

    done = []
    for j in range(NC):
        go("a0", own, left.at[c], (r, cx), j)
        go("a1", own, left.at[c], (r, yp), j)
        go("a2", own, left.at[c], (r, ym), j)
        go("b1", own, right.at[r], (zp, c), j)
        go("b2", own, right.at[r], (zm, c), j)
    for j in range(NC):
        go("f0", own, left.at[c], (r, ck), j)
    l0 = pltpu.make_async_copy(own, left.at[c], local_sem.at[0])
    l1 = pltpu.make_async_copy(own, right.at[r], local_sem.at[1])
    l0.start()
    l1.start()
    for j in range(NC):
        got("a0", j)
        go("b0", left.at[cx], right.at[r], (rx, cx), j)
        lf("a3", cx, (r, yp), j)
        lf("a4", cx, (r, ym), j)
        lf("f1", cx, (r, ck), j)
        got("b1", j)
        rt("b5", zm, (zp, c), j)
        got("a1", j)
        lf("a5", ym, (r, yp), j)
        lf("f2", ym, (r, ck), j)
        got("a2", j)
        lf("f3", yp, (r, ck), j)
    for j in range(NC):
        got("b0", j)
        rt("b3", rx, (zp, c), j)
        rt("b4", rx, (zm, c), j)
    for j in range(NC):
        got("a4", j)
        lf("a6", cxp, (r, ym), j)
        lf("f4", cxp, (r, ck), j)
        got("b4", j)
        rt("b6", rxp, (zm, c), j)
        got("a3", j)
        lf("f5", cxm, (r, ck), j)
        got("a5", j)
        lf("f6", y2, (r, ck), j)
    for j in range(NC):
        got("a6", j)
        lf("f7", yx2, (r, ck), j)
    for j in range(NC):
        for name in ("b2", "b3", "b5", "b6", "f0", "f1", "f2", "f3", "f4", "f5", "f6", "f7"):
            got(name, j)
    for cp in copies.values():
        cp.wait_send()
    l0.wait()
    l1.wait()


def gather(own):
    shape = own.shape
    n = 22 * NC
    return pl.pallas_call(
        gather_kernel,
        out_shape=(jax.ShapeDtypeStruct((16,) + shape, own.dtype), jax.ShapeDtypeStruct((8,) + shape, own.dtype)),
        in_specs=[pl.BlockSpec(memory_space=pltpu.VMEM)],
        out_specs=(pl.BlockSpec(memory_space=pl.ANY), pl.BlockSpec(memory_space=pl.ANY)),
        scratch_shapes=[pltpu.SemaphoreType.DMA((2,)), pltpu.SemaphoreType.DMA((n,)), pltpu.SemaphoreType.DMA((n,))],
        compiler_params=pltpu.CompilerParams(collective_id=0, has_side_effects=True),
    )(own)


def local(panels, stacks):
    left, right = gather(pack_tiles(panels[0, 0]))
    index = prep(stacks[:, 0, 0])
    out = make(8, 8)(*index, left.reshape(2048, 32, 128), right.reshape(1024, 32, 128))
    return out.reshape(1, 1, TPD, 1024)


def solution(mesh):
    in_specs = (P_("row", "col", None, None), P_(None, "row", "col", None, None))
    out_specs = P_("row", "col", None, None)
    return jax.shard_map(local, mesh=mesh, in_specs=in_specs, out_specs=out_specs, check_vma=False)
```

```python
import functools
import jax
import jax.numpy as jnp
from jax import lax
from jax.experimental import pallas as pl
from jax.sharding import PartitionSpec as P_
from jax.experimental.pallas import tpu as pltpu
TPD=512; STK=512
ROWS=520
PAD=2048+64
def make(H=4, UG=16, flags=None):
    def kernel(a_s,b_s,t_s,st,L,R,out,C0,C1,C2,C3,P,N):
        C=[C0,C1,C2,C3]
        h=pl.program_id(0)
        lg=lax.broadcasted_iota(jnp.int32,(32,128),1)//32
        keep=[lg==s for s in range(4)]
        lt2=lg<2
        zero=jnp.zeros((32,128),jnp.bfloat16)
        @pl.when(h==0)
        def _():
            P[...]=jnp.zeros(P.shape,jnp.float32)
            def z(i,_):
                for s in range(4):
                    C[s][pl.ds(pl.multiple_of(i*64,64),64),:]=jnp.zeros((64,128),jnp.float32)
                return 0
            lax.fori_loop(0,ROWS//2,z,0)
        for d in range(4):
            s_=[st[h*32+d*4+p] for p in range(4)]
            e_=[st[h*32+d*4+p+1] for p in range(4)]
            n=functools.reduce(jnp.maximum,[e-s for s,e in zip(s_,e_)])
            nb=(n+UG-1)//UG
            off=h*2048
            def compute(i,s_=s_,d=d,off=off):
                base=[s+off+i*UG for s in s_]
                for u in range(0,UG,2):
                    ls=[];rs=[]
                    for k in range(2):
                        av=[];bv=[]
                        for p in range(4):
                            ix=base[p]+(u+k)
                            av.append(L[a_s[ix]]); bv.append(R[b_s[ix]])
                        ls.append(jnp.where(lt2,jnp.where(keep[0],av[0],av[1]),jnp.where(keep[2],av[2],av[3])))
                        rs.append(jnp.concatenate([jnp.where(keep[(p+d)%4],bv[p],zero) for p in range(4)],axis=0))
                    o=jnp.dot(jnp.concatenate(ls,axis=0),jnp.concatenate(rs,axis=1),preferred_element_type=jnp.float32)
                    P[u]=o[:32,:128]; P[u+1]=o[32:,128:]
            def scatter(i,check,s_=s_,e_=e_,d=d,off=off):
                base=[s+off+i*UG for s in s_]
                end=[e+off for e in e_]
                for u in range(UG):
                    v=P[u]
                    for p in range(4):
                        ix=base[p]+u
                        t=t_s[ix]
                        if check: t=jnp.where(ix<end[p],t,TPD*32)
                        c=C[(p+d)%4]
                        w_=pl.ds(pl.multiple_of(t,32),32)
                        c[w_,:]=c[w_,:]+v
            def step(i,_):
                scatter(i-1,True); compute(i)
                return 0
            @pl.when(n>0)
            def _():
                compute(0)
                lax.fori_loop(1,nb,step,0)
                scatter(nb-1,True)
        @pl.when(h==H-1)
        def _():
            def masks(rows):
                g_=lax.broadcasted_iota(jnp.int32,(rows,128),1)//32
                return g_<2,(g_%2)==0
            n2,n1=masks(8)
            def fold(i,_):
                for w in range(16):
                    t=i*16+w
                    row=pl.multiple_of(t*32,32)
                    v=[]
                    for q in range(4):
                        x=[C[s][pl.ds(row+8*q,8),:] for s in range(4)]
                        v.append(jnp.where(n2,jnp.where(n1,x[0],x[1]),jnp.where(n1,x[2],x[3])))
                    z=[jnp.where(n2,v[k],v[k+2])+pltpu.roll(jnp.where(n2,v[k+2],v[k]),64,1) for k in range(2)]
                    x=jnp.where(n1,z[0],z[1]); y=jnp.where(n1,z[1],z[0])
                    N[pl.ds(pl.multiple_of(t*8,8),8),:]=x+jnp.where(n1,pltpu.roll(y,96,1),pltpu.roll(y,32,1))
                return 0
            lax.fori_loop(0,TPD//16,fold,0)
            m2,m1=masks(32)
            def swap(x,y,sh,mask):
                return jnp.where(mask,x,pltpu.roll(y,sh,1)), jnp.where(mask,pltpu.roll(x,128-sh,1),y)
            def fin(i,_):
                rows=pl.ds(pl.multiple_of(i*32,32),32)
                for hh in range(2):
                    v=[N[pl.ds(i*256+4*hh+w,32,stride=8),:] for w in range(4)]
                    v[0],v[2]=swap(v[0],v[2],64,m2); v[1],v[3]=swap(v[1],v[3],64,m2)
                    v[0],v[1]=swap(v[0],v[1],32,m1); v[2],v[3]=swap(v[2],v[3],32,m1)
                    for q in range(4):
                        c=2*q+hh
                        out[rows,c*128:(c+1)*128]=v[q]
                return 0
            lax.fori_loop(0,TPD//32,fin,0)
    return pl.pallas_call(kernel,
        out_shape=jax.ShapeDtypeStruct((TPD,1024),jnp.float32),
        grid_spec=pltpu.PrefetchScalarGridSpec(num_scalar_prefetch=4,grid=(H,),
            in_specs=[pl.BlockSpec((512,32,128),lambda h,*_:(h,0,0)),
                      pl.BlockSpec((256,32,128),lambda h,*_:(h,0,0))],
            out_specs=pl.BlockSpec((TPD,1024),lambda h,*_:(0,0)),
            scratch_shapes=[pltpu.VMEM((ROWS*32,128),jnp.float32)]*4+[pltpu.VMEM((UG,32,128),jnp.float32),pltpu.VMEM((TPD*8,128),jnp.float32)]),
        compiler_params=pltpu.CompilerParams(vmem_limit_bytes=62*2**20,dimension_semantics=("arbitrary",),flags=flags or {}))
def pack(x):
    s=x.shape[:-2]; n=len(s)
    return jnp.moveaxis(x.reshape(s+(128,4,32,32)),n+1,n+2).reshape(s+(128,32,128))
def prep(stacks):
    a,b,t=stacks[0],stacks[1],stacks[2]
    G=a.shape[0]
    g=lax.broadcasted_iota(jnp.int32,a.shape,0)
    cls=jnp.where(t<TPD,((b-a)&3)*4+(a&3),16)
    ap=a+(g&3)*TPD
    bp=b+((g>>1)&1)*TPD
    key=(cls<<26)|((ap>>2)<<17)|((bp>>2)<<9)|(t&511)
    key=key.reshape(G//4,4*STK)
    cl=cls.reshape(G//4,4*STK)
    st=jnp.sum((cl[:,:,None]<lax.broadcasted_iota(jnp.int32,(1,1,32),2)).astype(jnp.int32),axis=1)
    k=lax.sort(key,dimension=1,is_stable=False).reshape(-1)
    k=jnp.pad(k,(0,PAD))
    return (k>>17)&511,(k>>9)&255,(k&511)<<5,st.reshape(-1)

def pack_kernel(x, o, xf, of):
    lgq = lax.broadcasted_iota(jnp.int32, (128, 128), 1) // 32
    n2 = lgq < 2
    n1 = (lgq % 2) == 0

    def swap(x, y, sh, mask):
        return jnp.where(mask, x, pltpu.roll(y, sh, 1)), jnp.where(mask, pltpu.roll(x, 128 - sh, 1), y)

    for c in range(8):
        xf[...] = x[:, c * 128:(c + 1) * 128].astype(jnp.float32)
        v = [xf[pl.ds(q, 128, stride=4), :] for q in range(4)]
        v[0], v[2] = swap(v[0], v[2], 64, n2)
        v[1], v[3] = swap(v[1], v[3], 64, n2)
        v[0], v[1] = swap(v[0], v[1], 32, n1)
        v[2], v[3] = swap(v[2], v[3], 32, n1)
        for w in range(4):
            of[pl.ds(4 * c + w, 128, stride=32), :] = v[w]

    def cast(i, _):
        rows = pl.ds(pl.multiple_of(i * 512, 512), 512)
        o[rows, :] = of[rows, :].astype(jnp.bfloat16)
        return 0

    lax.fori_loop(0, 8, cast, 0)


def pack_tiles(x):
    return pl.pallas_call(
        pack_kernel,
        out_shape=jax.ShapeDtypeStruct((4096, 128), jnp.bfloat16),
        in_specs=[pl.BlockSpec(memory_space=pltpu.VMEM)],
        out_specs=pl.BlockSpec(memory_space=pltpu.VMEM),
        scratch_shapes=[pltpu.VMEM((512, 128), jnp.float32), pltpu.VMEM((4096, 128), jnp.float32)],
    )(x).reshape(128, 32, 128)
NC = 4


def gather_kernel(own, left, right, local_sem, send, recv):
    r = lax.axis_index("row"); c = lax.axis_index("col")
    xl = lax.rem(c // 2, 2); k = lax.rem(c, 2); xh = lax.rem(r, 2)
    yp, ym = lax.rem(c + 4, 16), lax.rem(c + 12, 16)
    cx, ck = c + 2 - 4 * xl, c + 1 - 2 * k
    cxp, cxm = lax.rem(cx + 4, 16), lax.rem(cx + 12, 16)
    zp, zm = lax.rem(r + 2, 8), lax.rem(r + 6, 8)
    rx = r + 1 - 2 * xh
    rxp, rxm = lax.rem(rx + 2, 8), lax.rem(rx + 6, 8)
    y2, yx2 = lax.rem(c + 8, 16), lax.rem(cx + 8, 16)
    barrier = pltpu.get_barrier_semaphore()
    for d in ((r, yp), (r, ym), (r, cx), (r, ck), (zp, c), (zm, c), (rx, cx)):
        pl.semaphore_signal(barrier, inc=1, device_id=d, device_id_type=pl.DeviceIdType.MESH)
    pl.semaphore_wait(barrier, 7)
    copies = {}
    rows = own.shape[0] // NC

    def go(name, src, dst, device, j):
        n = len(copies)
        piece = pl.ds(j * rows, rows)
        cp = pltpu.make_async_remote_copy(src_ref=src.at[piece], dst_ref=dst.at[piece], send_sem=send.at[n],
                                          recv_sem=recv.at[n], device_id=device, device_id_type=pl.DeviceIdType.MESH)
        cp.start()
        copies[name, j] = cp

    def lf(name, i, device, j):
        go(name, left.at[i], left.at[i], device, j)

    def rt(name, i, device, j):
        go(name, right.at[i], right.at[i], device, j)

    def got(name, j):
        copies[name, j].wait_recv()

    done = []
    for j in range(NC):
        go("a0", own, left.at[c], (r, cx), j)
        go("a1", own, left.at[c], (r, yp), j)
        go("a2", own, left.at[c], (r, ym), j)
        go("b1", own, right.at[r], (zp, c), j)
        go("b2", own, right.at[r], (zm, c), j)
    for j in range(NC):
        go("f0", own, left.at[c], (r, ck), j)
    l0 = pltpu.make_async_copy(own, left.at[c], local_sem.at[0])
    l1 = pltpu.make_async_copy(own, right.at[r], local_sem.at[1])
    l0.start()
    l1.start()
    for j in range(NC):
        got("a0", j)
        go("b0", left.at[cx], right.at[r], (rx, cx), j)
        lf("a3", cx, (r, yp), j)
        lf("a4", cx, (r, ym), j)
        lf("f1", cx, (r, ck), j)
        got("b1", j)
        rt("b5", zm, (zp, c), j)
        got("a1", j)
        lf("a5", ym, (r, yp), j)
        lf("f2", ym, (r, ck), j)
        got("a2", j)
        lf("f3", yp, (r, ck), j)
    for j in range(NC):
        got("b0", j)
        rt("b3", rx, (zp, c), j)
        rt("b4", rx, (zm, c), j)
    for j in range(NC):
        got("a4", j)
        lf("a6", cxp, (r, ym), j)
        lf("f4", cxp, (r, ck), j)
        got("b4", j)
        rt("b6", rxp, (zm, c), j)
        got("a3", j)
        lf("f5", cxm, (r, ck), j)
        got("a5", j)
        lf("f6", y2, (r, ck), j)
    for j in range(NC):
        got("a6", j)
        lf("f7", yx2, (r, ck), j)
    for j in range(NC):
        for name in ("b2", "b3", "b5", "b6", "f0", "f1", "f2", "f3", "f4", "f5", "f6", "f7"):
            got(name, j)
    for cp in copies.values():
        cp.wait_send()
    l0.wait()
    l1.wait()


def gather(own):
    shape = own.shape
    n = 22 * NC
    return pl.pallas_call(
        gather_kernel,
        out_shape=(jax.ShapeDtypeStruct((16,) + shape, own.dtype), jax.ShapeDtypeStruct((8,) + shape, own.dtype)),
        in_specs=[pl.BlockSpec(memory_space=pltpu.VMEM)],
        out_specs=(pl.BlockSpec(memory_space=pl.ANY), pl.BlockSpec(memory_space=pl.ANY)),
        scratch_shapes=[pltpu.SemaphoreType.DMA((2,)), pltpu.SemaphoreType.DMA((n,)), pltpu.SemaphoreType.DMA((n,))],
        compiler_params=pltpu.CompilerParams(collective_id=0, has_side_effects=True),
    )(own)


def local(panels, stacks):
    left, right = gather(pack_tiles(panels[0, 0]))
    index = prep(stacks[:, 0, 0])
    out = make(4, 16)(*index, left.reshape(2048, 32, 128), right.reshape(1024, 32, 128))
    return out.reshape(1, 1, TPD, 1024)


def solution(mesh):
    in_specs = (P_("row", "col", None, None), P_(None, "row", "col", None, None))
    out_specs = P_("row", "col", None, None)
    return jax.shard_map(local, mesh=mesh, in_specs=in_specs, out_specs=out_specs, check_vma=False)
```

```python
import functools
import jax
import jax.numpy as jnp
from jax import lax
from jax.experimental import pallas as pl
from jax.sharding import PartitionSpec as P_
from jax.experimental.pallas import tpu as pltpu
TPD=512; STK=512
ROWS=520
def make(H=4, UG=16, flags=None):
    def kernel(a_s,b_s,t_s,st,L,R,out,C0,C1,C2,C3,P,N):
        C=[C0,C1,C2,C3]
        h=pl.program_id(0)
        lg=lax.broadcasted_iota(jnp.int32,(32,128),1)//32
        keep=[lg==s for s in range(4)]
        lt2=lg<2
        zero=jnp.zeros((32,128),jnp.bfloat16)
        @pl.when(h==0)
        def _():
            P[...]=jnp.zeros(P.shape,jnp.float32)
            def z(i,_):
                for s in range(4):
                    C[s][pl.ds(pl.multiple_of(i*64,64),64),:]=jnp.zeros((64,128),jnp.float32)
                return 0
            lax.fori_loop(0,ROWS//2,z,0)
        for d in range(4):
            s_=[st[h*24+d*4+p,0] for p in range(4)]
            e_=[st[h*24+d*4+p+1,0] for p in range(4)]
            n=functools.reduce(jnp.maximum,[e-s for s,e in zip(s_,e_)])
            nb=(n+UG-1)//UG
            off=h*2048
            def compute(i,s_=s_,d=d,off=off):
                base=[s+off+i*UG for s in s_]
                for u in range(0,UG,2):
                    ls=[];rs=[]
                    for k in range(2):
                        av=[];bv=[]
                        for p in range(4):
                            ix=base[p]+(u+k)
                            av.append(L[a_s[ix]]); bv.append(R[b_s[ix]])
                        ls.append(jnp.where(lt2,jnp.where(keep[0],av[0],av[1]),jnp.where(keep[2],av[2],av[3])))
                        rs.append(jnp.concatenate([jnp.where(keep[(p+d)%4],bv[p],zero) for p in range(4)],axis=0))
                    o=jnp.dot(jnp.concatenate(ls,axis=0),jnp.concatenate(rs,axis=1),preferred_element_type=jnp.float32)
                    P[u]=o[:32,:128]; P[u+1]=o[32:,128:]
            def scatter(i,check,s_=s_,e_=e_,d=d,off=off):
                base=[s+off+i*UG for s in s_]
                end=[e+off for e in e_]
                for u in range(UG):
                    v=P[u]
                    for p in range(4):
                        ix=base[p]+u
                        t=t_s[ix]
                        if check: t=jnp.where(ix<end[p],t,TPD*32)
                        c=C[(p+d)%4]
                        w_=pl.ds(pl.multiple_of(t,32),32)
                        c[w_,:]=c[w_,:]+v
            def step(i,_):
                scatter(i-1,True); compute(i)
                return 0
            @pl.when(n>0)
            def _():
                compute(0)
                lax.fori_loop(1,nb,step,0)
                scatter(nb-1,True)
        @pl.when(h==H-1)
        def _():
            def masks(rows):
                g_=lax.broadcasted_iota(jnp.int32,(rows,128),1)//32
                return g_<2,(g_%2)==0
            n2,n1=masks(8)
            def fold(i,_):
                for w in range(16):
                    t=i*16+w
                    row=pl.multiple_of(t*32,32)
                    v=[]
                    for q in range(4):
                        x=[C[s][pl.ds(row+8*q,8),:] for s in range(4)]
                        v.append(jnp.where(n2,jnp.where(n1,x[0],x[1]),jnp.where(n1,x[2],x[3])))
                    z=[jnp.where(n2,v[k],v[k+2])+pltpu.roll(jnp.where(n2,v[k+2],v[k]),64,1) for k in range(2)]
                    x=jnp.where(n1,z[0],z[1]); y=jnp.where(n1,z[1],z[0])
                    N[pl.ds(pl.multiple_of(t*8,8),8),:]=x+jnp.where(n1,pltpu.roll(y,96,1),pltpu.roll(y,32,1))
                return 0
            lax.fori_loop(0,TPD//16,fold,0)
            m2,m1=masks(32)
            def swap(x,y,sh,mask):
                return jnp.where(mask,x,pltpu.roll(y,sh,1)), jnp.where(mask,pltpu.roll(x,128-sh,1),y)
            def fin(i,_):
                rows=pl.ds(pl.multiple_of(i*32,32),32)
                for hh in range(2):
                    v=[N[pl.ds(i*256+4*hh+w,32,stride=8),:] for w in range(4)]
                    v[0],v[2]=swap(v[0],v[2],64,m2); v[1],v[3]=swap(v[1],v[3],64,m2)
                    v[0],v[1]=swap(v[0],v[1],32,m1); v[2],v[3]=swap(v[2],v[3],32,m1)
                    for q in range(4):
                        c=2*q+hh
                        out[rows,c*128:(c+1)*128]=v[q]
                return 0
            lax.fori_loop(0,TPD//32,fin,0)
    return pl.pallas_call(kernel,
        out_shape=jax.ShapeDtypeStruct((TPD,1024),jnp.float32),
        grid_spec=pltpu.PrefetchScalarGridSpec(num_scalar_prefetch=4,grid=(H,),
            in_specs=[pl.BlockSpec((512,32,128),lambda h,*_:(h,0,0)),
                      pl.BlockSpec((256,32,128),lambda h,*_:(h,0,0))],
            out_specs=pl.BlockSpec((TPD,1024),lambda h,*_:(0,0)),
            scratch_shapes=[pltpu.VMEM((ROWS*32,128),jnp.float32)]*4+[pltpu.VMEM((UG,32,128),jnp.float32),pltpu.VMEM((TPD*8,128),jnp.float32)]),
        compiler_params=pltpu.CompilerParams(vmem_limit_bytes=62*2**20,dimension_semantics=("arbitrary",),flags=flags or {}))

def pack_kernel(x, o, xf, of):
    lgq = lax.broadcasted_iota(jnp.int32, (128, 128), 1) // 32
    n2 = lgq < 2
    n1 = (lgq % 2) == 0

    def swap(x, y, sh, mask):
        return jnp.where(mask, x, pltpu.roll(y, sh, 1)), jnp.where(mask, pltpu.roll(x, 128 - sh, 1), y)

    for c in range(8):
        xf[...] = x[:, c * 128:(c + 1) * 128].astype(jnp.float32)
        v = [xf[pl.ds(q, 128, stride=4), :] for q in range(4)]
        v[0], v[2] = swap(v[0], v[2], 64, n2)
        v[1], v[3] = swap(v[1], v[3], 64, n2)
        v[0], v[1] = swap(v[0], v[1], 32, n1)
        v[2], v[3] = swap(v[2], v[3], 32, n1)
        for w in range(4):
            of[pl.ds(4 * c + w, 128, stride=32), :] = v[w]

    def cast(i, _):
        rows = pl.ds(pl.multiple_of(i * 512, 512), 512)
        o[rows, :] = of[rows, :].astype(jnp.bfloat16)
        return 0

    lax.fori_loop(0, 8, cast, 0)


def pack_tiles(x):
    return pl.pallas_call(
        pack_kernel,
        out_shape=jax.ShapeDtypeStruct((4096, 128), jnp.bfloat16),
        in_specs=[pl.BlockSpec(memory_space=pltpu.VMEM)],
        out_specs=pl.BlockSpec(memory_space=pltpu.VMEM),
        scratch_shapes=[pltpu.VMEM((512, 128), jnp.float32), pltpu.VMEM((4096, 128), jnp.float32)],
    )(x).reshape(128, 32, 128)

LISTS = 4
SROWS = 88


def sort_stage_a(stk, m_s, cum_s, pos_s, val_s, st_o):
    a, b, t = stk[0], stk[1], stk[2]
    g = lax.broadcasted_iota(jnp.int32, (16, STK), 0)
    cls = jnp.where(t < TPD, ((b - a) & 3) * 4 + (a & 3), 16)
    ic = lax.broadcasted_iota(jnp.int32, (16, STK), 0)
    fields = (a >> 2, b >> 2, (t & 511) >> 1, (t & 1) + 2 * (g & 7))
    for k in range(16):
        m_s[16 * k:16 * k + 16, :] = (ic == cls[k:k + 1, :]).astype(jnp.float32).astype(jnp.bfloat16)
        v = jnp.zeros((16, STK), jnp.float32)
        for n, f in enumerate(fields):
            v = jnp.where(ic == n, f[k:k + 1, :].astype(jnp.float32), v)
        val_s[16 * k:16 * k + 16, :] = v.astype(jnp.bfloat16)
    upper = (lax.broadcasted_iota(jnp.int32, (STK, STK), 0) <= lax.broadcasted_iota(jnp.int32, (STK, STK), 1))
    cum_s[...] = jnp.dot(m_s[...], upper.astype(jnp.float32).astype(jnp.bfloat16), preferred_element_type=jnp.float32)
    ic1 = lax.broadcasted_iota(jnp.int32, (16, 128), 0)
    for q in range(LISTS):
        tots = [jnp.broadcast_to(cum_s[16 * (4 * q + k):16 * (4 * q + k) + 16, STK - 1:STK], (16, 128)) for k in range(4)]
        total = tots[0] + tots[1] + tots[2] + tots[3]
        start = jnp.zeros((16, 128), jnp.float32)
        for c in range(15):
            start = start + jnp.where(ic1 > c, jnp.broadcast_to(total[c:c + 1, :], (16, 128)), 0.0)
        st_o[q, 0:16, :] = start.astype(jnp.int32)
        live = jnp.broadcast_to(start[15:16, :] + total[15:16, :], (8, 128))
        st_o[q, 16:24, :] = live.astype(jnp.int32)
        base = start
        for k in range(4):
            r = 16 * (4 * q + k)
            w = m_s[r:r + 16, :].astype(jnp.float32) * (cum_s[r:r + 16, :] + base[:, 0:1])
            pos_s[4 * q + k:4 * q + k + 1, :] = jnp.sum(w, axis=0, keepdims=True)
            base = base + tots[k]


def sort_stage_b(k, pos_s, val_s, acc_s):
    q = k // 4
    pos = pos_s[k:k + 1, :].astype(jnp.int32)
    v = val_s[16 * k:16 * k + 16, :]

    def part(i, _):
        rows = lax.broadcasted_iota(jnp.int32, (256, STK), 0) + (i * 256 + 1)
        pick = (rows == pos).astype(jnp.float32).astype(jnp.bfloat16)
        o = lax.dot_general(v, pick, (((1,), (1,)), ((), ())), preferred_element_type=jnp.float32)
        cols = pl.ds(pl.multiple_of(i * 256, 256), 256)
        if k % 4 == 0:
            acc_s[q, :, cols] = o
        else:
            acc_s[q, :, cols] = acc_s[q, :, cols] + o
        return 0

    lax.fori_loop(0, 4 * STK // 256, part, 0)


def sort_stage_c(acc_s, ia, ib, it):
    for q in range(LISTS):
        f = [acc_s[q, n:n + 1, :].astype(jnp.int32) for n in range(4)]
        gg = f[3] >> 1
        av = (gg & 3) * 128 + f[0]
        bv = ((gg >> 1) & 1) * 128 + f[1]
        tv = (f[2] * 2 + (f[3] & 1)) * 32
        for k in range(16):
            sl = slice(128 * k, 128 * k + 128)
            ia[16 * q + k:16 * q + k + 1, :] = av[:, sl]
            ib[16 * q + k:16 * q + k + 1, :] = bv[:, sl]
            it[16 * q + k:16 * q + k + 1, :] = tv[:, sl]
    z = jnp.zeros((SROWS - 64, 128), jnp.int32)
    ia[64:SROWS, :] = z
    ib[64:SROWS, :] = z
    it[64:SROWS, :] = z


SORT_OUT = [jax.ShapeDtypeStruct((SROWS, 128), jnp.int32)] * 3 + [jax.ShapeDtypeStruct((LISTS, 24, 128), jnp.int32)]
SORT_SCRATCH = [pltpu.VMEM((256, STK), jnp.bfloat16), pltpu.VMEM((256, STK), jnp.float32), pltpu.VMEM((16, STK), jnp.float32),
                pltpu.VMEM((256, STK), jnp.bfloat16), pltpu.VMEM((LISTS, 16, 4 * STK), jnp.float32)]
NC = 4


def gather_kernel(own, stk, left, right, ia, ib, it, st_o, local_sem, send, recv, m_s, cum_s, pos_s, val_s, acc_s):
    r = lax.axis_index("row"); c = lax.axis_index("col")
    xl = lax.rem(c // 2, 2); k = lax.rem(c, 2); xh = lax.rem(r, 2)
    yp, ym = lax.rem(c + 4, 16), lax.rem(c + 12, 16)
    cx, ck = c + 2 - 4 * xl, c + 1 - 2 * k
    cxp, cxm = lax.rem(cx + 4, 16), lax.rem(cx + 12, 16)
    zp, zm = lax.rem(r + 2, 8), lax.rem(r + 6, 8)
    rx = r + 1 - 2 * xh
    rxp, rxm = lax.rem(rx + 2, 8), lax.rem(rx + 6, 8)
    y2, yx2 = lax.rem(c + 8, 16), lax.rem(cx + 8, 16)
    barrier = pltpu.get_barrier_semaphore()
    for d in ((r, yp), (r, ym), (r, cx), (r, ck), (zp, c), (zm, c), (rx, cx)):
        pl.semaphore_signal(barrier, inc=1, device_id=d, device_id_type=pl.DeviceIdType.MESH)
    pl.semaphore_wait(barrier, 7)
    copies = {}
    rows = own.shape[0] // NC

    def go(name, src, dst, device, j):
        n = len(copies)
        piece = pl.ds(j * rows, rows)
        cp = pltpu.make_async_remote_copy(src_ref=src.at[piece], dst_ref=dst.at[piece], send_sem=send.at[n],
                                          recv_sem=recv.at[n], device_id=device, device_id_type=pl.DeviceIdType.MESH)
        cp.start()
        copies[name, j] = cp

    def lf(name, i, device, j):
        go(name, left.at[i], left.at[i], device, j)

    def rt(name, i, device, j):
        go(name, right.at[i], right.at[i], device, j)

    def got(name, j):
        copies[name, j].wait_recv()

    done = []
    for j in range(NC):
        go("a0", own, left.at[c], (r, cx), j)
        go("a1", own, left.at[c], (r, yp), j)
        go("a2", own, left.at[c], (r, ym), j)
        go("b1", own, right.at[r], (zp, c), j)
        go("b2", own, right.at[r], (zm, c), j)
    for j in range(NC):
        go("f0", own, left.at[c], (r, ck), j)
    l0 = pltpu.make_async_copy(own, left.at[c], local_sem.at[0])
    l1 = pltpu.make_async_copy(own, right.at[r], local_sem.at[1])
    l0.start()
    l1.start()
    sort_stage_a(stk, m_s, cum_s, pos_s, val_s, st_o)
    for j in range(NC):
        got("a0", j)
        go("b0", left.at[cx], right.at[r], (rx, cx), j)
        lf("a3", cx, (r, yp), j)
        lf("a4", cx, (r, ym), j)
        lf("f1", cx, (r, ck), j)
        got("b1", j)
        rt("b5", zm, (zp, c), j)
        got("a1", j)
        lf("a5", ym, (r, yp), j)
        lf("f2", ym, (r, ck), j)
        got("a2", j)
        lf("f3", yp, (r, ck), j)
        sort_stage_b(j, pos_s, val_s, acc_s)
    for j in range(NC):
        got("b0", j)
        rt("b3", rx, (zp, c), j)
        rt("b4", rx, (zm, c), j)
        sort_stage_b(4 + j, pos_s, val_s, acc_s)
    for j in range(NC):
        got("a4", j)
        lf("a6", cxp, (r, ym), j)
        lf("f4", cxp, (r, ck), j)
        got("b4", j)
        rt("b6", rxp, (zm, c), j)
        sort_stage_b(8 + 2 * j, pos_s, val_s, acc_s)
        got("a3", j)
        lf("f5", cxm, (r, ck), j)
        got("a5", j)
        lf("f6", y2, (r, ck), j)
        sort_stage_b(9 + 2 * j, pos_s, val_s, acc_s)
    for j in range(NC):
        got("a6", j)
        lf("f7", yx2, (r, ck), j)
    sort_stage_c(acc_s, ia, ib, it)
    for j in range(NC):
        for name in ("b2", "b3", "b5", "b6", "f0", "f1", "f2", "f3", "f4", "f5", "f6", "f7"):
            got(name, j)
    for cp in copies.values():
        cp.wait_send()
    l0.wait()
    l1.wait()


def gather(own, stk):
    shape = own.shape
    n = 22 * NC
    return pl.pallas_call(
        gather_kernel,
        out_shape=(jax.ShapeDtypeStruct((16,) + shape, own.dtype), jax.ShapeDtypeStruct((8,) + shape, own.dtype), *SORT_OUT),
        in_specs=[pl.BlockSpec(memory_space=pltpu.VMEM)] * 2,
        out_specs=(pl.BlockSpec(memory_space=pl.ANY), pl.BlockSpec(memory_space=pl.ANY), *[pl.BlockSpec(memory_space=pltpu.VMEM)] * 4),
        scratch_shapes=[pltpu.SemaphoreType.DMA((2,)), pltpu.SemaphoreType.DMA((n,)), pltpu.SemaphoreType.DMA((n,))] + SORT_SCRATCH,
        compiler_params=pltpu.CompilerParams(collective_id=0, has_side_effects=True),
    )(own, stk)


def local(panels, stacks):
    left, right, ia, ib, it, starts = gather(pack_tiles(panels[0, 0]), stacks[:, 0, 0])
    out = make(4, 16)(ia.reshape(-1), ib.reshape(-1), it.reshape(-1), starts.reshape(-1, 128),
                      left.reshape(2048, 32, 128), right.reshape(1024, 32, 128))
    return out.reshape(1, 1, TPD, 1024)


def solution(mesh):
    in_specs = (P_("row", "col", None, None), P_(None, "row", "col", None, None))
    out_specs = P_("row", "col", None, None)
    return jax.shard_map(local, mesh=mesh, in_specs=in_specs, out_specs=out_specs, check_vma=False)
```

```python
import functools
import jax
import jax.numpy as jnp
from jax import lax
from jax.experimental import pallas as pl
from jax.sharding import PartitionSpec as P_
from jax.experimental.pallas import tpu as pltpu
TPD=512; STK=512
ROWS=520
def make(H=4, UG=16, flags=None):
    def kernel(a_s,b_s,t_s,st,L,R,out,C0,C1,C2,C3,P,N):
        C=[C0,C1,C2,C3]
        h=pl.program_id(0)
        lg=lax.broadcasted_iota(jnp.int32,(32,128),1)//32
        keep=[lg==s for s in range(4)]
        lt2=lg<2
        zero=jnp.zeros((32,128),jnp.bfloat16)
        @pl.when(h==0)
        def _():
            P[...]=jnp.zeros(P.shape,jnp.float32)
            def z(i,_):
                for s in range(4):
                    C[s][pl.ds(pl.multiple_of(i*64,64),64),:]=jnp.zeros((64,128),jnp.float32)
                return 0
            lax.fori_loop(0,ROWS//2,z,0)
        for d in range(4):
            s_=[st[h*24+d*4+p,0] for p in range(4)]
            e_=[st[h*24+d*4+p+1,0] for p in range(4)]
            n=functools.reduce(jnp.maximum,[e-s for s,e in zip(s_,e_)])
            nb=(n+UG-1)//UG
            off=h*2048
            def compute(i,s_=s_,d=d,off=off):
                base=[s+off+i*UG for s in s_]
                for u in range(0,UG,2):
                    ls=[];rs=[]
                    for k in range(2):
                        av=[];bv=[]
                        for p in range(4):
                            ix=base[p]+(u+k)
                            av.append(L[a_s[ix]]); bv.append(R[b_s[ix]])
                        ls.append(jnp.where(lt2,jnp.where(keep[0],av[0],av[1]),jnp.where(keep[2],av[2],av[3])))
                        rs.append(jnp.concatenate([jnp.where(keep[(p+d)%4],bv[p],zero) for p in range(4)],axis=0))
                    o=jnp.dot(jnp.concatenate(ls,axis=0),jnp.concatenate(rs,axis=1),preferred_element_type=jnp.float32)
                    P[u]=o[:32,:128]; P[u+1]=o[32:,128:]
            def scatter(i,check,s_=s_,e_=e_,d=d,off=off):
                base=[s+off+i*UG for s in s_]
                end=[e+off for e in e_]
                for u in range(UG):
                    v=P[u]
                    for p in range(4):
                        ix=base[p]+u
                        t=t_s[ix]
                        if check: t=jnp.where(ix<end[p],t,TPD*32)
                        c=C[(p+d)%4]
                        w_=pl.ds(pl.multiple_of(t,32),32)
                        c[w_,:]=c[w_,:]+v
            def step(i,_):
                scatter(i-1,True); compute(i)
                return 0
            @pl.when(n>0)
            def _():
                compute(0)
                lax.fori_loop(1,nb,step,0)
                scatter(nb-1,True)
        @pl.when(h==H-1)
        def _():
            def masks(rows):
                g_=lax.broadcasted_iota(jnp.int32,(rows,128),1)//32
                return g_<2,(g_%2)==0
            n2,n1=masks(8)
            g8=lax.broadcasted_iota(jnp.int32,(8,128),1)//32
            sel=[(g8==0)|(g8==3),n2]
            def fold(i,_):
                for w in range(16):
                    t=i*16+w
                    row=pl.multiple_of(t*32,32)
                    v=[]
                    for q in range(4):
                        x=[C[s][pl.ds(row+8*q,8),:] for s in range(4)]
                        v.append(jnp.where(n2,jnp.where(n1,x[0],x[1]),jnp.where(n1,x[2],x[3])))
                    z=[jnp.where(sel[k],v[k],v[k+2])+pltpu.roll(jnp.where(sel[k],v[k+2],v[k]),64,1) for k in range(2)]
                    N[pl.ds(pl.multiple_of(t*8,8),8),:]=jnp.where(n1,z[0],z[1])+pltpu.roll(jnp.where(n1,z[1],z[0]),32,1)
                return 0
            lax.fori_loop(0,TPD//16,fold,0)
            m2,m1=masks(32)
            def swap(x,y,sh,mask):
                return jnp.where(mask,x,pltpu.roll(y,sh,1)), jnp.where(mask,pltpu.roll(x,128-sh,1),y)
            def fin(i,_):
                rows=pl.ds(pl.multiple_of(i*32,32),32)
                for hh in range(2):
                    v=[N[pl.ds(i*256+4*hh+w,32,stride=8),:] for w in range(4)]
                    v[0],v[2]=swap(v[0],v[2],64,m2); v[1],v[3]=swap(v[1],v[3],64,m2)
                    v[0],v[1]=swap(v[0],v[1],32,m1); v[2],v[3]=swap(v[2],v[3],32,m1)
                    for q in range(4):
                        c=2*q+hh
                        out[rows,c*128:(c+1)*128]=v[q]
                return 0
            lax.fori_loop(0,TPD//32,fin,0)
    return pl.pallas_call(kernel,
        out_shape=jax.ShapeDtypeStruct((TPD,1024),jnp.float32),
        grid_spec=pltpu.PrefetchScalarGridSpec(num_scalar_prefetch=4,grid=(H,),
            in_specs=[pl.BlockSpec((512,32,128),lambda h,*_:(h,0,0)),
                      pl.BlockSpec((256,32,128),lambda h,*_:(h,0,0))],
            out_specs=pl.BlockSpec((TPD,1024),lambda h,*_:(0,0)),
            scratch_shapes=[pltpu.VMEM((ROWS*32,128),jnp.float32)]*4+[pltpu.VMEM((UG,32,128),jnp.float32),pltpu.VMEM((TPD*8,128),jnp.float32)]),
        compiler_params=pltpu.CompilerParams(vmem_limit_bytes=62*2**20,dimension_semantics=("arbitrary",),flags=flags or {}))

def pack_kernel(x, o, xf, of):
    lgq = lax.broadcasted_iota(jnp.int32, (128, 128), 1) // 32
    n2 = lgq < 2
    n1 = (lgq % 2) == 0

    def swap(x, y, sh, mask):
        return jnp.where(mask, x, pltpu.roll(y, sh, 1)), jnp.where(mask, pltpu.roll(x, 128 - sh, 1), y)

    for c in range(8):
        xf[...] = x[:, c * 128:(c + 1) * 128].astype(jnp.float32)
        v = [xf[pl.ds(q, 128, stride=4), :] for q in range(4)]
        v[0], v[2] = swap(v[0], v[2], 64, n2)
        v[1], v[3] = swap(v[1], v[3], 64, n2)
        v[0], v[1] = swap(v[0], v[1], 32, n1)
        v[2], v[3] = swap(v[2], v[3], 32, n1)
        for w in range(4):
            of[pl.ds(4 * c + w, 128, stride=32), :] = v[w]

    def cast(i, _):
        rows = pl.ds(pl.multiple_of(i * 512, 512), 512)
        o[rows, :] = of[rows, :].astype(jnp.bfloat16)
        return 0

    lax.fori_loop(0, 8, cast, 0)


def pack_tiles(x):
    return pl.pallas_call(
        pack_kernel,
        out_shape=jax.ShapeDtypeStruct((4096, 128), jnp.bfloat16),
        in_specs=[pl.BlockSpec(memory_space=pltpu.VMEM)],
        out_specs=pl.BlockSpec(memory_space=pltpu.VMEM),
        scratch_shapes=[pltpu.VMEM((512, 128), jnp.float32), pltpu.VMEM((4096, 128), jnp.float32)],
    )(x).reshape(128, 32, 128)

LISTS = 4
SROWS = 88


def sort_stage_a(stk, m_s, cum_s, pos_s, val_s, st_o):
    a, b, t = stk[0], stk[1], stk[2]
    g = lax.broadcasted_iota(jnp.int32, (16, STK), 0)
    cls = jnp.where(t < TPD, ((b - a) & 3) * 4 + (a & 3), 16)
    ic = lax.broadcasted_iota(jnp.int32, (16, STK), 0)
    fields = (a >> 2, b >> 2, (t & 511) >> 1, (t & 1) + 2 * (g & 7))
    for k in range(16):
        m_s[16 * k:16 * k + 16, :] = (ic == cls[k:k + 1, :]).astype(jnp.float32).astype(jnp.bfloat16)
        v = jnp.zeros((16, STK), jnp.float32)
        for n, f in enumerate(fields):
            v = jnp.where(ic == n, f[k:k + 1, :].astype(jnp.float32), v)
        val_s[16 * k:16 * k + 16, :] = v.astype(jnp.bfloat16)
    upper = (lax.broadcasted_iota(jnp.int32, (STK, STK), 0) <= lax.broadcasted_iota(jnp.int32, (STK, STK), 1))
    cum_s[...] = jnp.dot(m_s[...], upper.astype(jnp.float32).astype(jnp.bfloat16), preferred_element_type=jnp.float32)
    ic1 = lax.broadcasted_iota(jnp.int32, (16, 128), 0)
    for q in range(LISTS):
        tots = [jnp.broadcast_to(cum_s[16 * (4 * q + k):16 * (4 * q + k) + 16, STK - 1:STK], (16, 128)) for k in range(4)]
        total = tots[0] + tots[1] + tots[2] + tots[3]
        start = jnp.zeros((16, 128), jnp.float32)
        for c in range(15):
            start = start + jnp.where(ic1 > c, jnp.broadcast_to(total[c:c + 1, :], (16, 128)), 0.0)
        st_o[q, 0:16, :] = start.astype(jnp.int32)
        live = jnp.broadcast_to(start[15:16, :] + total[15:16, :], (8, 128))
        st_o[q, 16:24, :] = live.astype(jnp.int32)
        base = start
        for k in range(4):
            r = 16 * (4 * q + k)
            w = m_s[r:r + 16, :].astype(jnp.float32) * (cum_s[r:r + 16, :] + base[:, 0:1])
            pos_s[4 * q + k:4 * q + k + 1, :] = jnp.sum(w, axis=0, keepdims=True)
            base = base + tots[k]


def sort_stage_b(k, pos_s, val_s, acc_s):
    q = k // 4
    pos = pos_s[k:k + 1, :].astype(jnp.int32)
    v = val_s[16 * k:16 * k + 16, :]

    def part(i, _):
        rows = lax.broadcasted_iota(jnp.int32, (256, STK), 0) + (i * 256 + 1)
        pick = (rows == pos).astype(jnp.float32).astype(jnp.bfloat16)
        o = lax.dot_general(v, pick, (((1,), (1,)), ((), ())), preferred_element_type=jnp.float32)
        cols = pl.ds(pl.multiple_of(i * 256, 256), 256)
        if k % 4 == 0:
            acc_s[q, :, cols] = o
        else:
            acc_s[q, :, cols] = acc_s[q, :, cols] + o
        return 0

    lax.fori_loop(0, 4 * STK // 256, part, 0)


def sort_stage_c(acc_s, ia, ib, it):
    for q in range(LISTS):
        f = [acc_s[q, n:n + 1, :].astype(jnp.int32) for n in range(4)]
        gg = f[3] >> 1
        av = (gg & 3) * 128 + f[0]
        bv = ((gg >> 1) & 1) * 128 + f[1]
        tv = (f[2] * 2 + (f[3] & 1)) * 32
        for k in range(16):
            sl = slice(128 * k, 128 * k + 128)
            ia[16 * q + k:16 * q + k + 1, :] = av[:, sl]
            ib[16 * q + k:16 * q + k + 1, :] = bv[:, sl]
            it[16 * q + k:16 * q + k + 1, :] = tv[:, sl]
    z = jnp.zeros((SROWS - 64, 128), jnp.int32)
    ia[64:SROWS, :] = z
    ib[64:SROWS, :] = z
    it[64:SROWS, :] = z


SORT_OUT = [jax.ShapeDtypeStruct((SROWS, 128), jnp.int32)] * 3 + [jax.ShapeDtypeStruct((LISTS, 24, 128), jnp.int32)]
SORT_SCRATCH = [pltpu.VMEM((256, STK), jnp.bfloat16), pltpu.VMEM((256, STK), jnp.float32), pltpu.VMEM((16, STK), jnp.float32),
                pltpu.VMEM((256, STK), jnp.bfloat16), pltpu.VMEM((LISTS, 16, 4 * STK), jnp.float32)]
NC = 4


def gather_kernel(own, stk, left, right, relay, ia, ib, it, st_o, local_sem, send, recv, m_s, cum_s, pos_s, val_s, acc_s):
    r = lax.axis_index("row"); c = lax.axis_index("col")
    xl = lax.rem(c // 2, 2); k = lax.rem(c, 2); xh = lax.rem(r, 2)
    yp, ym = lax.rem(c + 4, 16), lax.rem(c + 12, 16)
    cx, ck = c + 2 - 4 * xl, c + 1 - 2 * k
    cxp, cxm = lax.rem(cx + 4, 16), lax.rem(cx + 12, 16)
    zp, zm = lax.rem(r + 2, 8), lax.rem(r + 6, 8)
    rx = r + 1 - 2 * xh
    rxp, rxm = lax.rem(rx + 2, 8), lax.rem(rx + 6, 8)
    y2, yx2 = lax.rem(c + 8, 16), lax.rem(cx + 8, 16)
    barrier = pltpu.get_barrier_semaphore()
    for d in ((r, yp), (r, ym), (r, cx), (r, ck), (zp, c), (zm, c), (rx, cx)):
        pl.semaphore_signal(barrier, inc=1, device_id=d, device_id_type=pl.DeviceIdType.MESH)
    pl.semaphore_wait(barrier, 7)
    copies = {}
    rows = own.shape[0] // NC

    def go(name, src, dst, device, j):
        n = len(copies)
        piece = pl.ds(j * rows, rows)
        cp = pltpu.make_async_remote_copy(src_ref=src.at[piece], dst_ref=dst.at[piece], send_sem=send.at[n],
                                          recv_sem=recv.at[n], device_id=device, device_id_type=pl.DeviceIdType.MESH)
        cp.start()
        copies[name, j] = cp

    def lf(name, i, device, j):
        go(name, left.at[i], left.at[i], device, j)

    def rt(name, i, device, j):
        go(name, right.at[i], right.at[i], device, j)

    def got(name, j):
        copies[name, j].wait_recv()

    r2, rx2 = lax.rem(r + 4, 8), lax.rem(rx + 4, 8)

    def raw(name, src, dst, device, j):
        n = len(copies)
        cp = pltpu.make_async_remote_copy(src_ref=src, dst_ref=dst, send_sem=send.at[n], recv_sem=recv.at[n],
                                          device_id=device, device_id_type=pl.DeviceIdType.MESH)
        cp.start()
        copies[name, j] = cp

    def piece(j):
        return pl.ds(j * rows, rows)

    for j in range(NC):
        go("a0", own, left.at[c], (r, cx), j)
        go("a1", own, left.at[c], (r, yp), j)
        go("a2", own, left.at[c], (r, ym), j)
        go("b1", own, right.at[r], (zp, c), j)
        go("b2", own, right.at[r], (zm, c), j)
    for j in range(NC):
        go("f0", own, left.at[c], (r, ck), j)
    l0 = pltpu.make_async_copy(own, left.at[c], local_sem.at[0])
    l1 = pltpu.make_async_copy(own, right.at[r], local_sem.at[1])
    l0.start()
    l1.start()
    sort_stage_a(stk, m_s, cum_s, pos_s, val_s, st_o)
    for j in range(NC):
        got("a0", j)
        go("b0", left.at[cx], right.at[r], (rx, cx), j)
        lf("f1", cx, (r, ck), j)
        got("a1", j)
        got("a2", j)
        if j < 2:
            lf("a5", ym, (r, yp), j)
        else:
            lf("a5", yp, (r, ym), j)
        lf("a3", cx, (r, yp), j)
        lf("a4", cx, (r, ym), j)
        lf("f2", ym, (r, ck), j)
        lf("f3", yp, (r, ck), j)
        got("b1", j)
        got("b2", j)
        if j < 3:
            rt("b5", zm, (zp, c), j)
        else:
            rt("b5", zp, (zm, c), j)
        sort_stage_b(j, pos_s, val_s, acc_s)
    for j in range(NC):
        got("b0", j)
        rt("b3", rx, (zp, c), j)
        rt("b4", rx, (zm, c), j)
        sort_stage_b(4 + j, pos_s, val_s, acc_s)
    got("b5", 0)
    raw("r", right.at[r2].at[piece(0)], relay.at[0], (r, cx), 0)
    got("b5", 1)
    raw("r", right.at[r2].at[piece(1)], relay.at[1], (rx, cx), 1)
    for j in range(NC):
        got("a5", j)
        lf("a6", y2, (r, cx), j)
        lf("f6", y2, (r, ck), j)
        if j == 1:
            got("r", 0)
            raw("b6", relay.at[0], right.at[r2].at[piece(0)], (rx, cx), 0)
            got("r", 1)
            raw("b6", relay.at[1], right.at[rx2].at[piece(1)], (r, cx), 1)
        got("a4", j)
        lf("f4", cxp, (r, ck), j)
        if j >= 2:
            got("b4", j)
            rt("b6", rxp, (zm, c), j)
        got("a3", j)
        lf("f5", cxm, (r, ck), j)
        sort_stage_b(8 + 2 * j, pos_s, val_s, acc_s)
        sort_stage_b(9 + 2 * j, pos_s, val_s, acc_s)
    for j in range(NC):
        got("a6", j)
        lf("f7", yx2, (r, ck), j)
    sort_stage_c(acc_s, ia, ib, it)
    got("b4", 0)
    got("b4", 1)
    got("b5", 2)
    got("b5", 3)
    for j in range(NC):
        for name in ("b3", "b6", "f0", "f1", "f2", "f3", "f4", "f5", "f6", "f7"):
            got(name, j)
    for cp in copies.values():
        cp.wait_send()
    l0.wait()
    l1.wait()


def gather(own, stk):
    shape = own.shape
    n = 90
    return pl.pallas_call(
        gather_kernel,
        out_shape=(jax.ShapeDtypeStruct((16,) + shape, own.dtype), jax.ShapeDtypeStruct((8,) + shape, own.dtype),
                   jax.ShapeDtypeStruct((2, shape[0] // NC) + shape[1:], own.dtype), *SORT_OUT),
        in_specs=[pl.BlockSpec(memory_space=pltpu.VMEM)] * 2,
        out_specs=(pl.BlockSpec(memory_space=pl.ANY),) * 3 + (pl.BlockSpec(memory_space=pltpu.VMEM),) * 4,
        scratch_shapes=[pltpu.SemaphoreType.DMA((2,)), pltpu.SemaphoreType.DMA((n,)), pltpu.SemaphoreType.DMA((n,))] + SORT_SCRATCH,
        compiler_params=pltpu.CompilerParams(collective_id=0, has_side_effects=True),
    )(own, stk)


def local(panels, stacks):
    left, right, _, ia, ib, it, starts = gather(pack_tiles(panels[0, 0]), stacks[:, 0, 0])
    out = make(4, 24)(ia.reshape(-1), ib.reshape(-1), it.reshape(-1), starts.reshape(-1, 128),
                      left.reshape(2048, 32, 128), right.reshape(1024, 32, 128))
    return out.reshape(1, 1, TPD, 1024)


def solution(mesh):
    in_specs = (P_("row", "col", None, None), P_(None, "row", "col", None, None))
    out_specs = P_("row", "col", None, None)
    return jax.shard_map(local, mesh=mesh, in_specs=in_specs, out_specs=out_specs, check_vma=False)
```

```python
import functools
import jax
import jax.numpy as jnp
from jax import lax
from jax.experimental import pallas as pl
from jax.sharding import PartitionSpec as P_
from jax.experimental.pallas import tpu as pltpu
TPD=512; STK=512
ROWS=520
def make(H=4, UG=16, flags=None):
    def kernel(a_s,b_s,t_s,st,L,R,out,C0,C1,C2,C3,P,N):
        C=[C0,C1,C2,C3]
        h=pl.program_id(0)
        lg=lax.broadcasted_iota(jnp.int32,(32,128),1)//32
        keep=[lg==s for s in range(4)]
        lt2=lg<2
        zero=jnp.zeros((32,128),jnp.bfloat16)
        @pl.when(h==0)
        def _():
            P[...]=jnp.zeros(P.shape,jnp.float32)
            def z(i,_):
                for s in range(4):
                    C[s][pl.ds(pl.multiple_of(i*64,64),64),:]=jnp.zeros((64,128),jnp.float32)
                return 0
            lax.fori_loop(0,ROWS//2,z,0,unroll=4)
        for d in range(4):
            s_=[st[h*24+d*4+p,0] for p in range(4)]
            e_=[st[h*24+d*4+p+1,0] for p in range(4)]
            n=functools.reduce(jnp.maximum,[e-s for s,e in zip(s_,e_)])
            nb=(n+UG-1)//UG
            off=h*2048
            def compute(i,s_=s_,d=d,off=off):
                base=[s+off+i*UG for s in s_]
                for u in range(0,UG,2):
                    ls=[];rs=[]
                    for k in range(2):
                        av=[];bv=[]
                        for p in range(4):
                            ix=base[p]+(u+k)
                            av.append(L[a_s[ix]]); bv.append(R[b_s[ix]])
                        ls.append(jnp.where(lt2,jnp.where(keep[0],av[0],av[1]),jnp.where(keep[2],av[2],av[3])))
                        rs.append(jnp.concatenate([jnp.where(keep[(p+d)%4],bv[p],zero) for p in range(4)],axis=0))
                    o=jnp.dot(jnp.concatenate(ls,axis=0),jnp.concatenate(rs,axis=1),preferred_element_type=jnp.float32)
                    P[u]=o[:32,:128]; P[u+1]=o[32:,128:]
            def scatter(i,check,s_=s_,e_=e_,d=d,off=off):
                base=[s+off+i*UG for s in s_]
                end=[e+off for e in e_]
                for u in range(UG):
                    v=P[u]
                    for p in range(4):
                        ix=base[p]+u
                        t=t_s[ix]
                        if check: t=jnp.where(ix<end[p],t,TPD*32)
                        c=C[(p+d)%4]
                        w_=pl.ds(pl.multiple_of(t,32),32)
                        c[w_,:]=c[w_,:]+v
            def step(i,_):
                scatter(i-1,True); compute(i)
                return 0
            @pl.when(n>0)
            def _():
                compute(0)
                lax.fori_loop(1,nb,step,0)
                scatter(nb-1,True)
        @pl.when(h==H-1)
        def _():
            def masks(rows):
                g_=lax.broadcasted_iota(jnp.int32,(rows,128),1)//32
                return g_<2,(g_%2)==0
            n2,n1=masks(8)
            g8=lax.broadcasted_iota(jnp.int32,(8,128),1)//32
            sel=[(g8==0)|(g8==3),n2]
            def fold(i,_):
                for w in range(32):
                    t=i*32+w
                    row=pl.multiple_of(t*32,32)
                    v=[]
                    for q in range(4):
                        x=[C[s][pl.ds(row+8*q,8),:] for s in range(4)]
                        v.append(jnp.where(n2,jnp.where(n1,x[0],x[1]),jnp.where(n1,x[2],x[3])))
                    z=[jnp.where(sel[k],v[k],v[k+2])+pltpu.roll(jnp.where(sel[k],v[k+2],v[k]),64,1) for k in range(2)]
                    N[pl.ds(pl.multiple_of(t*8,8),8),:]=jnp.where(n1,z[0],z[1])+pltpu.roll(jnp.where(n1,z[1],z[0]),32,1)
                return 0
            lax.fori_loop(0,TPD//32,fold,0,unroll=2)
            m2,m1=masks(32)
            def swap(x,y,sh,mask):
                return jnp.where(mask,x,pltpu.roll(y,sh,1)), jnp.where(mask,pltpu.roll(x,128-sh,1),y)
            def fin(i,_):
                rows=pl.ds(pl.multiple_of(i*32,32),32)
                for hh in range(2):
                    v=[N[pl.ds(i*256+4*hh+w,32,stride=8),:] for w in range(4)]
                    v[0],v[2]=swap(v[0],v[2],64,m2); v[1],v[3]=swap(v[1],v[3],64,m2)
                    v[0],v[1]=swap(v[0],v[1],32,m1); v[2],v[3]=swap(v[2],v[3],32,m1)
                    for q in range(4):
                        c=2*q+hh
                        out[rows,c*128:(c+1)*128]=v[q]
                return 0
            lax.fori_loop(0,TPD//32,fin,0,unroll=2)
    return pl.pallas_call(kernel,
        out_shape=jax.ShapeDtypeStruct((TPD,1024),jnp.float32),
        grid_spec=pltpu.PrefetchScalarGridSpec(num_scalar_prefetch=4,grid=(H,),
            in_specs=[pl.BlockSpec((512,32,128),lambda h,*_:(h,0,0)),
                      pl.BlockSpec((256,32,128),lambda h,*_:(h,0,0))],
            out_specs=pl.BlockSpec((TPD,1024),lambda h,*_:(0,0)),
            scratch_shapes=[pltpu.VMEM((ROWS*32,128),jnp.float32)]*4+[pltpu.VMEM((UG,32,128),jnp.float32),pltpu.VMEM((TPD*8,128),jnp.float32)]),
        compiler_params=pltpu.CompilerParams(vmem_limit_bytes=62*2**20,dimension_semantics=("arbitrary",),flags=flags or {}))

def pack_kernel(x, o, xf, of):
    lgq = lax.broadcasted_iota(jnp.int32, (128, 128), 1) // 32
    n2 = lgq < 2
    n1 = (lgq % 2) == 0

    def swap(x, y, sh, mask):
        return jnp.where(mask, x, pltpu.roll(y, sh, 1)), jnp.where(mask, pltpu.roll(x, 128 - sh, 1), y)

    for c in range(8):
        xf[...] = x[:, c * 128:(c + 1) * 128].astype(jnp.float32)
        v = [xf[pl.ds(q, 128, stride=4), :] for q in range(4)]
        v[0], v[2] = swap(v[0], v[2], 64, n2)
        v[1], v[3] = swap(v[1], v[3], 64, n2)
        v[0], v[1] = swap(v[0], v[1], 32, n1)
        v[2], v[3] = swap(v[2], v[3], 32, n1)
        for w in range(4):
            of[pl.ds(4 * c + w, 128, stride=32), :] = v[w]

    def cast(i, _):
        rows = pl.ds(pl.multiple_of(i * 512, 512), 512)
        o[rows, :] = of[rows, :].astype(jnp.bfloat16)
        return 0

    lax.fori_loop(0, 8, cast, 0)


def pack_tiles(x):
    return pl.pallas_call(
        pack_kernel,
        out_shape=jax.ShapeDtypeStruct((4096, 128), jnp.bfloat16),
        in_specs=[pl.BlockSpec(memory_space=pltpu.VMEM)],
        out_specs=pl.BlockSpec(memory_space=pltpu.VMEM),
        scratch_shapes=[pltpu.VMEM((512, 128), jnp.float32), pltpu.VMEM((4096, 128), jnp.float32)],
    )(x).reshape(128, 32, 128)

LISTS = 4
SROWS = 88


def sort_stage_a(stk, m_s, cum_s, pos_s, val_s, st_o):
    a, b, t = stk[0], stk[1], stk[2]
    g = lax.broadcasted_iota(jnp.int32, (16, STK), 0)
    cls = jnp.where(t < TPD, ((b - a) & 3) * 4 + (a & 3), 16)
    ic = lax.broadcasted_iota(jnp.int32, (16, STK), 0)
    fields = (a >> 2, b >> 2, (t & 511) >> 1, (t & 1) + 2 * (g & 7))
    for k in range(16):
        m_s[16 * k:16 * k + 16, :] = (ic == cls[k:k + 1, :]).astype(jnp.float32).astype(jnp.bfloat16)
        v = jnp.zeros((16, STK), jnp.float32)
        for n, f in enumerate(fields):
            v = jnp.where(ic == n, f[k:k + 1, :].astype(jnp.float32), v)
        val_s[16 * k:16 * k + 16, :] = v.astype(jnp.bfloat16)
    upper = (lax.broadcasted_iota(jnp.int32, (STK, STK), 0) <= lax.broadcasted_iota(jnp.int32, (STK, STK), 1))
    cum_s[...] = jnp.dot(m_s[...], upper.astype(jnp.float32).astype(jnp.bfloat16), preferred_element_type=jnp.float32)
    ic1 = lax.broadcasted_iota(jnp.int32, (16, 128), 0)
    for q in range(LISTS):
        tots = [jnp.broadcast_to(cum_s[16 * (4 * q + k):16 * (4 * q + k) + 16, STK - 1:STK], (16, 128)) for k in range(4)]
        total = tots[0] + tots[1] + tots[2] + tots[3]
        start = jnp.zeros((16, 128), jnp.float32)
        for c in range(15):
            start = start + jnp.where(ic1 > c, jnp.broadcast_to(total[c:c + 1, :], (16, 128)), 0.0)
        st_o[q, 0:16, :] = start.astype(jnp.int32)
        live = jnp.broadcast_to(start[15:16, :] + total[15:16, :], (8, 128))
        st_o[q, 16:24, :] = live.astype(jnp.int32)
        base = start
        for k in range(4):
            r = 16 * (4 * q + k)
            w = m_s[r:r + 16, :].astype(jnp.float32) * (cum_s[r:r + 16, :] + base[:, 0:1])
            pos_s[4 * q + k:4 * q + k + 1, :] = jnp.sum(w, axis=0, keepdims=True)
            base = base + tots[k]


def sort_stage_b(k, pos_s, val_s, acc_s):
    q = k // 4
    pos = pos_s[k:k + 1, :].astype(jnp.int32)
    v = val_s[16 * k:16 * k + 16, :]

    def part(i, _):
        rows = lax.broadcasted_iota(jnp.int32, (256, STK), 0) + (i * 256 + 1)
        pick = (rows == pos).astype(jnp.float32).astype(jnp.bfloat16)
        o = lax.dot_general(v, pick, (((1,), (1,)), ((), ())), preferred_element_type=jnp.float32)
        cols = pl.ds(pl.multiple_of(i * 256, 256), 256)
        if k % 4 == 0:
            acc_s[q, :, cols] = o
        else:
            acc_s[q, :, cols] = acc_s[q, :, cols] + o
        return 0

    lax.fori_loop(0, 4 * STK // 256, part, 0)


def sort_stage_c(acc_s, ia, ib, it):
    for q in range(LISTS):
        f = [acc_s[q, n:n + 1, :].astype(jnp.int32) for n in range(4)]
        gg = f[3] >> 1
        av = (gg & 3) * 128 + f[0]
        bv = ((gg >> 1) & 1) * 128 + f[1]
        tv = (f[2] * 2 + (f[3] & 1)) * 32
        for k in range(16):
            sl = slice(128 * k, 128 * k + 128)
            ia[16 * q + k:16 * q + k + 1, :] = av[:, sl]
            ib[16 * q + k:16 * q + k + 1, :] = bv[:, sl]
            it[16 * q + k:16 * q + k + 1, :] = tv[:, sl]
    z = jnp.zeros((SROWS - 64, 128), jnp.int32)
    ia[64:SROWS, :] = z
    ib[64:SROWS, :] = z
    it[64:SROWS, :] = z


SORT_OUT = [jax.ShapeDtypeStruct((SROWS, 128), jnp.int32)] * 3 + [jax.ShapeDtypeStruct((LISTS, 24, 128), jnp.int32)]
SORT_SCRATCH = [pltpu.VMEM((256, STK), jnp.bfloat16), pltpu.VMEM((256, STK), jnp.float32), pltpu.VMEM((16, STK), jnp.float32),
                pltpu.VMEM((256, STK), jnp.bfloat16), pltpu.VMEM((LISTS, 16, 4 * STK), jnp.float32)]
NC = 4


def gather_kernel(own, stk, left, right, relay, ia, ib, it, st_o, local_sem, send, recv, m_s, cum_s, pos_s, val_s, acc_s):
    r = lax.axis_index("row"); c = lax.axis_index("col")
    xl = lax.rem(c // 2, 2); k = lax.rem(c, 2); xh = lax.rem(r, 2)
    yp, ym = lax.rem(c + 4, 16), lax.rem(c + 12, 16)
    cx, ck = c + 2 - 4 * xl, c + 1 - 2 * k
    cxp, cxm = lax.rem(cx + 4, 16), lax.rem(cx + 12, 16)
    zp, zm = lax.rem(r + 2, 8), lax.rem(r + 6, 8)
    rx = r + 1 - 2 * xh
    rxp, rxm = lax.rem(rx + 2, 8), lax.rem(rx + 6, 8)
    y2, yx2 = lax.rem(c + 8, 16), lax.rem(cx + 8, 16)
    barrier = pltpu.get_barrier_semaphore()
    for d in ((r, yp), (r, ym), (r, cx), (r, ck), (zp, c), (zm, c), (rx, cx)):
        pl.semaphore_signal(barrier, inc=1, device_id=d, device_id_type=pl.DeviceIdType.MESH)
    pl.semaphore_wait(barrier, 7)
    copies = {}
    rows = own.shape[0] // NC

    def go(name, src, dst, device, j):
        n = len(copies)
        piece = pl.ds(j * rows, rows)
        cp = pltpu.make_async_remote_copy(src_ref=src.at[piece], dst_ref=dst.at[piece], send_sem=send.at[n],
                                          recv_sem=recv.at[n], device_id=device, device_id_type=pl.DeviceIdType.MESH)
        cp.start()
        copies[name, j] = cp

    def lf(name, i, device, j):
        go(name, left.at[i], left.at[i], device, j)

    def rt(name, i, device, j):
        go(name, right.at[i], right.at[i], device, j)

    def got(name, j):
        copies[name, j].wait_recv()

    r2, rx2 = lax.rem(r + 4, 8), lax.rem(rx + 4, 8)

    def raw(name, src, dst, device, j):
        n = len(copies)
        cp = pltpu.make_async_remote_copy(src_ref=src, dst_ref=dst, send_sem=send.at[n], recv_sem=recv.at[n],
                                          device_id=device, device_id_type=pl.DeviceIdType.MESH)
        cp.start()
        copies[name, j] = cp

    def piece(j):
        return pl.ds(j * rows, rows)

    for j in range(NC):
        go("a0", own, left.at[c], (r, cx), j)
        go("a1", own, left.at[c], (r, yp), j)
        go("a2", own, left.at[c], (r, ym), j)
        go("b1", own, right.at[r], (zp, c), j)
        go("b2", own, right.at[r], (zm, c), j)
    for j in range(NC):
        go("f0", own, left.at[c], (r, ck), j)
    l0 = pltpu.make_async_copy(own, left.at[c], local_sem.at[0])
    l1 = pltpu.make_async_copy(own, right.at[r], local_sem.at[1])
    l0.start()
    l1.start()
    sort_stage_a(stk, m_s, cum_s, pos_s, val_s, st_o)
    for j in range(NC):
        got("a0", j)
        go("b0", left.at[cx], right.at[r], (rx, cx), j)
        lf("f1", cx, (r, ck), j)
        got("a1", j)
        got("a2", j)
        if j < 2:
            lf("a5", ym, (r, yp), j)
        else:
            lf("a5", yp, (r, ym), j)
        lf("a3", cx, (r, yp), j)
        lf("a4", cx, (r, ym), j)
        lf("f2", ym, (r, ck), j)
        lf("f3", yp, (r, ck), j)
        got("b1", j)
        got("b2", j)
        if j < 3:
            rt("b5", zm, (zp, c), j)
        else:
            rt("b5", zp, (zm, c), j)
        sort_stage_b(2 * j, pos_s, val_s, acc_s)
        sort_stage_b(2 * j + 1, pos_s, val_s, acc_s)
    for j in range(NC):
        got("b0", j)
        rt("b3", rx, (zp, c), j)
        rt("b4", rx, (zm, c), j)
        sort_stage_b(8 + j, pos_s, val_s, acc_s)
    got("b5", 0)
    raw("r", right.at[r2].at[piece(0)], relay.at[0], (r, cx), 0)
    got("b5", 1)
    raw("r", right.at[r2].at[piece(1)], relay.at[1], (rx, cx), 1)
    for j in range(NC):
        got("a5", j)
        lf("a6", y2, (r, cx), j)
        lf("f6", y2, (r, ck), j)
        if j == 1:
            got("r", 0)
            raw("b6", relay.at[0], right.at[r2].at[piece(0)], (rx, cx), 0)
            got("r", 1)
            raw("b6", relay.at[1], right.at[rx2].at[piece(1)], (r, cx), 1)
        got("a4", j)
        lf("f4", cxp, (r, ck), j)
        if j >= 2:
            got("b4", j)
            rt("b6", rxp, (zm, c), j)
        got("a3", j)
        lf("f5", cxm, (r, ck), j)
        if j < 2:
            sort_stage_b(12 + 2 * j, pos_s, val_s, acc_s)
            sort_stage_b(13 + 2 * j, pos_s, val_s, acc_s)
        if j == 1:
            sort_stage_c(acc_s, ia, ib, it)
    for j in range(NC):
        got("a6", j)
        lf("f7", yx2, (r, ck), j)
    got("b4", 0)
    got("b4", 1)
    got("b5", 2)
    got("b5", 3)
    for j in range(NC):
        for name in ("b3", "b6", "f0", "f1", "f2", "f3", "f4", "f5", "f6", "f7"):
            got(name, j)
    for cp in copies.values():
        cp.wait_send()
    l0.wait()
    l1.wait()


def gather(own, stk):
    shape = own.shape
    n = 90
    return pl.pallas_call(
        gather_kernel,
        out_shape=(jax.ShapeDtypeStruct((16,) + shape, own.dtype), jax.ShapeDtypeStruct((8,) + shape, own.dtype),
                   jax.ShapeDtypeStruct((2, shape[0] // NC) + shape[1:], own.dtype), *SORT_OUT),
        in_specs=[pl.BlockSpec(memory_space=pltpu.VMEM)] * 2,
        out_specs=(pl.BlockSpec(memory_space=pl.ANY),) * 3 + (pl.BlockSpec(memory_space=pltpu.VMEM),) * 4,
        scratch_shapes=[pltpu.SemaphoreType.DMA((2,)), pltpu.SemaphoreType.DMA((n,)), pltpu.SemaphoreType.DMA((n,))] + SORT_SCRATCH,
        compiler_params=pltpu.CompilerParams(collective_id=0, has_side_effects=True),
    )(own, stk)


def local(panels, stacks):
    left, right, _, ia, ib, it, starts = gather(pack_tiles(panels[0, 0]), stacks[:, 0, 0])
    out = make(4, 24)(ia.reshape(-1), ib.reshape(-1), it.reshape(-1), starts.reshape(-1, 128),
                      left.reshape(2048, 32, 128), right.reshape(1024, 32, 128))
    return out.reshape(1, 1, TPD, 1024)


def solution(mesh):
    in_specs = (P_("row", "col", None, None), P_(None, "row", "col", None, None))
    out_specs = P_("row", "col", None, None)
    return jax.shard_map(local, mesh=mesh, in_specs=in_specs, out_specs=out_specs, check_vma=False)
```

```python
import functools
import jax
import jax.numpy as jnp
from jax import lax
from jax.experimental import pallas as pl
from jax.sharding import PartitionSpec as P_
from jax.experimental.pallas import tpu as pltpu
TPD=512; STK=512
ROWS=520
def make(H=4, UG=16, flags=None):
    def kernel(a_s,b_s,t_s,st,L,R,out,C0,C1,C2,C3,P,N):
        C=[C0,C1,C2,C3]
        h=pl.program_id(0)
        lg=lax.broadcasted_iota(jnp.int32,(32,128),1)//32
        keep=[lg==s for s in range(4)]
        lt2=lg<2
        zero=jnp.zeros((32,128),jnp.bfloat16)
        @pl.when(h==0)
        def _():
            P[...]=jnp.zeros(P.shape,jnp.float32)
            def z(i,_):
                for s in range(4):
                    C[s][pl.ds(pl.multiple_of(i*64,64),64),:]=jnp.zeros((64,128),jnp.float32)
                return 0
            lax.fori_loop(0,ROWS//2,z,0,unroll=4)
        for d in range(4):
            s_=[st[h*24+d*4+p,0] for p in range(4)]
            e_=[st[h*24+d*4+p+1,0] for p in range(4)]
            n=functools.reduce(jnp.maximum,[e-s for s,e in zip(s_,e_)])
            nb=(n+UG-1)//UG
            off=h*2048
            def compute(i,s_=s_,d=d,off=off):
                base=[s+off+i*UG for s in s_]
                for u in range(0,UG,2):
                    ls=[];rs=[]
                    for k in range(2):
                        av=[];bv=[]
                        for p in range(4):
                            ix=base[p]+(u+k)
                            av.append(L[a_s[ix]]); bv.append(R[b_s[ix]])
                        ls.append(jnp.where(lt2,jnp.where(keep[0],av[0],av[1]),jnp.where(keep[2],av[2],av[3])))
                        rs.append(jnp.concatenate([jnp.where(keep[(p+d)%4],bv[p],zero) for p in range(4)],axis=0))
                    o=jnp.dot(jnp.concatenate(ls,axis=0),jnp.concatenate(rs,axis=1),preferred_element_type=jnp.float32)
                    P[u]=o[:32,:128]; P[u+1]=o[32:,128:]
            def scatter(i,check,s_=s_,e_=e_,d=d,off=off):
                base=[s+off+i*UG for s in s_]
                end=[e+off for e in e_]
                for u in range(UG):
                    v=P[u]
                    for p in range(4):
                        ix=base[p]+u
                        t=t_s[ix]
                        if check: t=jnp.where(ix<end[p],t,TPD*32)
                        c=C[(p+d)%4]
                        w_=pl.ds(pl.multiple_of(t,32),32)
                        c[w_,:]=c[w_,:]+v
            def step(i,_):
                scatter(i-1,True); compute(i)
                return 0
            @pl.when(n>0)
            def _():
                compute(0)
                lax.fori_loop(1,nb,step,0)
                scatter(nb-1,True)
        @pl.when(h==H-1)
        def _():
            def masks(rows):
                g_=lax.broadcasted_iota(jnp.int32,(rows,128),1)//32
                return g_<2,(g_%2)==0
            n2,n1=masks(8)
            g8=lax.broadcasted_iota(jnp.int32,(8,128),1)//32
            sel=[(g8==0)|(g8==3),n2]
            def fold(i,_):
                for w in range(32):
                    t=i*32+w
                    row=pl.multiple_of(t*32,32)
                    v=[]
                    for q in range(4):
                        x=[C[s][pl.ds(row+8*q,8),:] for s in range(4)]
                        v.append(jnp.where(n2,jnp.where(n1,x[0],x[1]),jnp.where(n1,x[2],x[3])))
                    z=[jnp.where(sel[k],v[k],v[k+2])+pltpu.roll(jnp.where(sel[k],v[k+2],v[k]),64,1) for k in range(2)]
                    N[pl.ds(pl.multiple_of(t*8,8),8),:]=jnp.where(n1,z[0],z[1])+pltpu.roll(jnp.where(n1,z[1],z[0]),32,1)
                return 0
            lax.fori_loop(0,TPD//32,fold,0)
            m2,m1=masks(32)
            def swap(x,y,sh,mask):
                return jnp.where(mask,x,pltpu.roll(y,sh,1)), jnp.where(mask,pltpu.roll(x,128-sh,1),y)
            def fin(i,_):
                rows=pl.ds(pl.multiple_of(i*32,32),32)
                for hh in range(2):
                    v=[N[pl.ds(i*256+4*hh+w,32,stride=8),:] for w in range(4)]
                    v[0],v[2]=swap(v[0],v[2],64,m2); v[1],v[3]=swap(v[1],v[3],64,m2)
                    v[0],v[1]=swap(v[0],v[1],32,m1); v[2],v[3]=swap(v[2],v[3],32,m1)
                    for q in range(4):
                        c=2*q+hh
                        out[rows,c*128:(c+1)*128]=v[q]
                return 0
            lax.fori_loop(0,TPD//32,fin,0,unroll=2)
    return pl.pallas_call(kernel,
        out_shape=jax.ShapeDtypeStruct((TPD,1024),jnp.float32),
        grid_spec=pltpu.PrefetchScalarGridSpec(num_scalar_prefetch=4,grid=(H,),
            in_specs=[pl.BlockSpec((512,32,128),lambda h,*_:(h,0,0)),
                      pl.BlockSpec((256,32,128),lambda h,*_:(h,0,0))],
            out_specs=pl.BlockSpec((TPD,1024),lambda h,*_:(0,0)),
            scratch_shapes=[pltpu.VMEM((ROWS*32,128),jnp.float32)]*4+[pltpu.VMEM((UG,32,128),jnp.float32),pltpu.VMEM((TPD*8,128),jnp.float32)]),
        compiler_params=pltpu.CompilerParams(vmem_limit_bytes=62*2**20,dimension_semantics=("arbitrary",),flags=flags or {}))

def pack_kernel(x, o, xf, of):
    lgq = lax.broadcasted_iota(jnp.int32, (128, 128), 1) // 32
    n2 = lgq < 2
    n1 = (lgq % 2) == 0

    def swap(x, y, sh, mask):
        return jnp.where(mask, x, pltpu.roll(y, sh, 1)), jnp.where(mask, pltpu.roll(x, 128 - sh, 1), y)

    for c in range(8):
        xf[...] = x[:, c * 128:(c + 1) * 128].astype(jnp.float32)
        v = [xf[pl.ds(q, 128, stride=4), :] for q in range(4)]
        v[0], v[2] = swap(v[0], v[2], 64, n2)
        v[1], v[3] = swap(v[1], v[3], 64, n2)
        v[0], v[1] = swap(v[0], v[1], 32, n1)
        v[2], v[3] = swap(v[2], v[3], 32, n1)
        for w in range(4):
            of[pl.ds(4 * c + w, 128, stride=32), :] = v[w]

    def cast(i, _):
        rows = pl.ds(pl.multiple_of(i * 512, 512), 512)
        o[rows, :] = of[rows, :].astype(jnp.bfloat16)
        return 0

    lax.fori_loop(0, 8, cast, 0)


def pack_tiles(x):
    return pl.pallas_call(
        pack_kernel,
        out_shape=jax.ShapeDtypeStruct((4096, 128), jnp.bfloat16),
        in_specs=[pl.BlockSpec(memory_space=pltpu.VMEM)],
        out_specs=pl.BlockSpec(memory_space=pltpu.VMEM),
        scratch_shapes=[pltpu.VMEM((512, 128), jnp.float32), pltpu.VMEM((4096, 128), jnp.float32)],
    )(x).reshape(128, 32, 128)

LISTS = 4
SROWS = 88


def sort_stage_a(stk, m_s, cum_s, pos_s, val_s, st_o):
    a, b, t = stk[0], stk[1], stk[2]
    g = lax.broadcasted_iota(jnp.int32, (16, STK), 0)
    cls = jnp.where(t < TPD, ((b - a) & 3) * 4 + (a & 3), 16)
    ic = lax.broadcasted_iota(jnp.int32, (16, STK), 0)
    fields = (a >> 2, b >> 2, (t & 511) >> 1, (t & 1) + 2 * (g & 7))
    for k in range(16):
        m_s[16 * k:16 * k + 16, :] = (ic == cls[k:k + 1, :]).astype(jnp.float32).astype(jnp.bfloat16)
        v = jnp.zeros((16, STK), jnp.float32)
        for n, f in enumerate(fields):
            v = jnp.where(ic == n, f[k:k + 1, :].astype(jnp.float32), v)
        val_s[16 * k:16 * k + 16, :] = v.astype(jnp.bfloat16)
    upper = (lax.broadcasted_iota(jnp.int32, (STK, STK), 0) <= lax.broadcasted_iota(jnp.int32, (STK, STK), 1))
    cum_s[...] = jnp.dot(m_s[...], upper.astype(jnp.float32).astype(jnp.bfloat16), preferred_element_type=jnp.float32)
    ic1 = lax.broadcasted_iota(jnp.int32, (16, 128), 0)
    for q in range(LISTS):
        tots = [jnp.broadcast_to(cum_s[16 * (4 * q + k):16 * (4 * q + k) + 16, STK - 1:STK], (16, 128)) for k in range(4)]
        total = tots[0] + tots[1] + tots[2] + tots[3]
        start = jnp.zeros((16, 128), jnp.float32)
        for c in range(15):
            start = start + jnp.where(ic1 > c, jnp.broadcast_to(total[c:c + 1, :], (16, 128)), 0.0)
        st_o[q, 0:16, :] = start.astype(jnp.int32)
        live = jnp.broadcast_to(start[15:16, :] + total[15:16, :], (8, 128))
        st_o[q, 16:24, :] = live.astype(jnp.int32)
        base = start
        for k in range(4):
            r = 16 * (4 * q + k)
            w = m_s[r:r + 16, :].astype(jnp.float32) * (cum_s[r:r + 16, :] + base[:, 0:1])
            pos_s[4 * q + k:4 * q + k + 1, :] = jnp.sum(w, axis=0, keepdims=True)
            base = base + tots[k]


def sort_stage_b(k, pos_s, val_s, acc_s):
    q = k // 4
    pos = pos_s[k:k + 1, :].astype(jnp.int32)
    v = val_s[16 * k:16 * k + 16, :]

    def part(i, _):
        rows = lax.broadcasted_iota(jnp.int32, (256, STK), 0) + (i * 256 + 1)
        pick = (rows == pos).astype(jnp.float32).astype(jnp.bfloat16)
        o = lax.dot_general(v, pick, (((1,), (1,)), ((), ())), preferred_element_type=jnp.float32)
        cols = pl.ds(pl.multiple_of(i * 256, 256), 256)
        if k % 4 == 0:
            acc_s[q, :, cols] = o
        else:
            acc_s[q, :, cols] = acc_s[q, :, cols] + o
        return 0

    lax.fori_loop(0, 4 * STK // 256, part, 0)


def sort_stage_c(acc_s, ia, ib, it):
    for q in range(LISTS):
        f = [acc_s[q, n:n + 1, :].astype(jnp.int32) for n in range(4)]
        gg = f[3] >> 1
        av = (gg & 3) * 128 + f[0]
        bv = ((gg >> 1) & 1) * 128 + f[1]
        tv = (f[2] * 2 + (f[3] & 1)) * 32
        for k in range(16):
            sl = slice(128 * k, 128 * k + 128)
            ia[16 * q + k:16 * q + k + 1, :] = av[:, sl]
            ib[16 * q + k:16 * q + k + 1, :] = bv[:, sl]
            it[16 * q + k:16 * q + k + 1, :] = tv[:, sl]
    z = jnp.zeros((SROWS - 64, 128), jnp.int32)
    ia[64:SROWS, :] = z
    ib[64:SROWS, :] = z
    it[64:SROWS, :] = z


SORT_OUT = [jax.ShapeDtypeStruct((SROWS, 128), jnp.int32)] * 3 + [jax.ShapeDtypeStruct((LISTS, 24, 128), jnp.int32)]
SORT_SCRATCH = [pltpu.VMEM((256, STK), jnp.bfloat16), pltpu.VMEM((256, STK), jnp.float32), pltpu.VMEM((16, STK), jnp.float32),
                pltpu.VMEM((256, STK), jnp.bfloat16), pltpu.VMEM((LISTS, 16, 4 * STK), jnp.float32)]
NC = 4


def gather_kernel(own, stk, left, right, relay, ia, ib, it, st_o, local_sem, send, recv, m_s, cum_s, pos_s, val_s, acc_s):
    r = lax.axis_index("row"); c = lax.axis_index("col")
    xl = lax.rem(c // 2, 2); k = lax.rem(c, 2); xh = lax.rem(r, 2)
    yp, ym = lax.rem(c + 4, 16), lax.rem(c + 12, 16)
    cx, ck = c + 2 - 4 * xl, c + 1 - 2 * k
    cxp, cxm = lax.rem(cx + 4, 16), lax.rem(cx + 12, 16)
    zp, zm = lax.rem(r + 2, 8), lax.rem(r + 6, 8)
    rx = r + 1 - 2 * xh
    rxp, rxm = lax.rem(rx + 2, 8), lax.rem(rx + 6, 8)
    y2, yx2 = lax.rem(c + 8, 16), lax.rem(cx + 8, 16)
    barrier = pltpu.get_barrier_semaphore()
    for d in ((r, yp), (r, ym), (r, cx), (r, ck), (zp, c), (zm, c), (rx, cx)):
        pl.semaphore_signal(barrier, inc=1, device_id=d, device_id_type=pl.DeviceIdType.MESH)
    pl.semaphore_wait(barrier, 7)
    copies = {}
    rows = own.shape[0] // NC

    def go(name, src, dst, device, j):
        n = len(copies)
        piece = pl.ds(j * rows, rows)
        cp = pltpu.make_async_remote_copy(src_ref=src.at[piece], dst_ref=dst.at[piece], send_sem=send.at[n],
                                          recv_sem=recv.at[n], device_id=device, device_id_type=pl.DeviceIdType.MESH)
        cp.start()
        copies[name, j] = cp

    def lf(name, i, device, j):
        go(name, left.at[i], left.at[i], device, j)

    def rt(name, i, device, j):
        go(name, right.at[i], right.at[i], device, j)

    def got(name, j):
        copies[name, j].wait_recv()

    r2, rx2 = lax.rem(r + 4, 8), lax.rem(rx + 4, 8)

    def raw(name, src, dst, device, j):
        n = len(copies)
        cp = pltpu.make_async_remote_copy(src_ref=src, dst_ref=dst, send_sem=send.at[n], recv_sem=recv.at[n],
                                          device_id=device, device_id_type=pl.DeviceIdType.MESH)
        cp.start()
        copies[name, j] = cp

    def piece(j):
        return pl.ds(j * rows, rows)

    for j in range(NC):
        go("a0", own, left.at[c], (r, cx), j)
        go("a1", own, left.at[c], (r, yp), j)
        go("a2", own, left.at[c], (r, ym), j)
        go("b1", own, right.at[r], (zp, c), j)
        go("b2", own, right.at[r], (zm, c), j)
    for j in range(NC):
        go("f0", own, left.at[c], (r, ck), j)
    l0 = pltpu.make_async_copy(own, left.at[c], local_sem.at[0])
    l1 = pltpu.make_async_copy(own, right.at[r], local_sem.at[1])
    l0.start()
    l1.start()
    sort_stage_a(stk, m_s, cum_s, pos_s, val_s, st_o)
    for j in range(NC):
        got("a0", j)
        go("b0", left.at[cx], right.at[r], (rx, cx), j)
        lf("f1", cx, (r, ck), j)
        got("a1", j)
        got("a2", j)
        if j < 2:
            lf("a5", ym, (r, yp), j)
        else:
            lf("a5", yp, (r, ym), j)
        lf("a3", cx, (r, yp), j)
        lf("a4", cx, (r, ym), j)
        lf("f2", ym, (r, ck), j)
        lf("f3", yp, (r, ck), j)
        got("b1", j)
        got("b2", j)
        if j < 3:
            rt("b5", zm, (zp, c), j)
        else:
            rt("b5", zp, (zm, c), j)
    for j in range(NC):
        got("b0", j)
        rt("b3", rx, (zp, c), j)
        rt("b4", rx, (zm, c), j)
        sort_stage_b(2 * j, pos_s, val_s, acc_s)
        sort_stage_b(2 * j + 1, pos_s, val_s, acc_s)
    got("b5", 0)
    raw("r", right.at[r2].at[piece(0)], relay.at[0], (r, cx), 0)
    got("b5", 1)
    raw("r", right.at[r2].at[piece(1)], relay.at[1], (rx, cx), 1)
    for j in range(NC):
        got("a5", j)
        lf("a6", y2, (r, cx), j)
        lf("f6", y2, (r, ck), j)
        if j == 1:
            got("r", 0)
            raw("b6", relay.at[0], right.at[r2].at[piece(0)], (rx, cx), 0)
            got("r", 1)
            raw("b6", relay.at[1], right.at[rx2].at[piece(1)], (r, cx), 1)
        got("a4", j)
        lf("f4", cxp, (r, ck), j)
        if j >= 2:
            got("b4", j)
            rt("b6", rxp, (zm, c), j)
        got("a3", j)
        lf("f5", cxm, (r, ck), j)
        sort_stage_b(8 + 2 * j, pos_s, val_s, acc_s)
        sort_stage_b(9 + 2 * j, pos_s, val_s, acc_s)
    for j in range(NC):
        got("a6", j)
        lf("f7", yx2, (r, ck), j)
    sort_stage_c(acc_s, ia, ib, it)
    got("b4", 0)
    got("b4", 1)
    got("b5", 2)
    got("b5", 3)
    for j in range(NC):
        for name in ("b3", "b6", "f0", "f1", "f2", "f3", "f4", "f5", "f6", "f7"):
            got(name, j)
    for cp in copies.values():
        cp.wait_send()
    l0.wait()
    l1.wait()


def gather(own, stk):
    shape = own.shape
    n = 90
    return pl.pallas_call(
        gather_kernel,
        out_shape=(jax.ShapeDtypeStruct((16,) + shape, own.dtype), jax.ShapeDtypeStruct((8,) + shape, own.dtype),
                   jax.ShapeDtypeStruct((2, shape[0] // NC) + shape[1:], own.dtype), *SORT_OUT),
        in_specs=[pl.BlockSpec(memory_space=pltpu.VMEM)] * 2,
        out_specs=(pl.BlockSpec(memory_space=pl.ANY),) * 3 + (pl.BlockSpec(memory_space=pltpu.VMEM),) * 4,
        scratch_shapes=[pltpu.SemaphoreType.DMA((2,)), pltpu.SemaphoreType.DMA((n,)), pltpu.SemaphoreType.DMA((n,))] + SORT_SCRATCH,
        compiler_params=pltpu.CompilerParams(collective_id=0, has_side_effects=True),
    )(own, stk)


def local(panels, stacks):
    left, right, _, ia, ib, it, starts = gather(pack_tiles(panels[0, 0]), stacks[:, 0, 0])
    out = make(4, 24)(ia.reshape(-1), ib.reshape(-1), it.reshape(-1), starts.reshape(-1, 128),
                      left.reshape(2048, 32, 128), right.reshape(1024, 32, 128))
    return out.reshape(1, 1, TPD, 1024)


def solution(mesh):
    in_specs = (P_("row", "col", None, None), P_(None, "row", "col", None, None))
    out_specs = P_("row", "col", None, None)
    return jax.shard_map(local, mesh=mesh, in_specs=in_specs, out_specs=out_specs, check_vma=False)
```

```python
import functools
import jax
import jax.numpy as jnp
from jax import lax
from jax.experimental import pallas as pl
from jax.sharding import PartitionSpec as P_
from jax.experimental.pallas import tpu as pltpu
TPD=512; STK=512
ROWS=520
def make(H=4, UG=16, flags=None):
    def kernel(a_s,b_s,t_s,st,L,R,out,C0,C1,C2,C3,P,N):
        C=[C0,C1,C2,C3]
        h=pl.program_id(0)
        lg=lax.broadcasted_iota(jnp.int32,(32,128),1)//32
        keep=[lg==s for s in range(4)]
        lt2=lg<2
        zero=jnp.zeros((32,128),jnp.bfloat16)
        @pl.when(h==0)
        def _():
            P[...]=jnp.zeros(P.shape,jnp.float32)
            def z(i,_):
                for s in range(4):
                    C[s][pl.ds(pl.multiple_of(i*64,64),64),:]=jnp.zeros((64,128),jnp.float32)
                return 0
            lax.fori_loop(0,ROWS//2,z,0,unroll=4)
        for d in range(4):
            s_=[st[h*24+d*4+p,0] for p in range(4)]
            e_=[st[h*24+d*4+p+1,0] for p in range(4)]
            n=functools.reduce(jnp.maximum,[e-s for s,e in zip(s_,e_)])
            nb=(n+UG-1)//UG
            off=h*2048
            def compute(i,s_=s_,d=d,off=off):
                base=[s+off+i*UG for s in s_]
                for u in range(0,UG,2):
                    ls=[];rs=[]
                    for k in range(2):
                        av=[];bv=[]
                        for p in range(4):
                            ix=base[p]+(u+k)
                            av.append(L[a_s[ix]]); bv.append(R[b_s[ix]])
                        ls.append(jnp.where(lt2,jnp.where(keep[0],av[0],av[1]),jnp.where(keep[2],av[2],av[3])))
                        rs.append(jnp.concatenate([jnp.where(keep[(p+d)%4],bv[p],zero) for p in range(4)],axis=0))
                    o=jnp.dot(jnp.concatenate(ls,axis=0),jnp.concatenate(rs,axis=1),preferred_element_type=jnp.float32)
                    P[u]=o[:32,:128]; P[u+1]=o[32:,128:]
            def scatter(i,check,s_=s_,e_=e_,d=d,off=off):
                base=[s+off+i*UG for s in s_]
                end=[e+off for e in e_]
                for u in range(UG):
                    v=P[u]
                    for p in range(4):
                        ix=base[p]+u
                        t=t_s[ix]
                        if check: t=jnp.where(ix<end[p],t,TPD*32)
                        c=C[(p+d)%4]
                        w_=pl.ds(pl.multiple_of(t,32),32)
                        c[w_,:]=c[w_,:]+v
            def step(i,_):
                scatter(i-1,True); compute(i)
                return 0
            @pl.when(n>0)
            def _():
                compute(0)
                lax.fori_loop(1,nb,step,0)
                scatter(nb-1,True)
        @pl.when(h==H-1)
        def _():
            def masks(rows):
                g_=lax.broadcasted_iota(jnp.int32,(rows,128),1)//32
                return g_<2,(g_%2)==0
            n2,n1=masks(8)
            g8=lax.broadcasted_iota(jnp.int32,(8,128),1)//32
            sel=[(g8==0)|(g8==3),n2]
            def fold(i,_):
                for w in range(32):
                    t=i*32+w
                    row=pl.multiple_of(t*32,32)
                    v=[]
                    for q in range(4):
                        x=[C[s][pl.ds(row+8*q,8),:] for s in range(4)]
                        v.append(jnp.where(n2,jnp.where(n1,x[0],x[1]),jnp.where(n1,x[2],x[3])))
                    z=[jnp.where(sel[k],v[k],v[k+2])+pltpu.roll(jnp.where(sel[k],v[k+2],v[k]),64,1) for k in range(2)]
                    N[pl.ds(pl.multiple_of(t*8,8),8),:]=jnp.where(n1,z[0],z[1])+pltpu.roll(jnp.where(n1,z[1],z[0]),32,1)
                return 0
            lax.fori_loop(0,TPD//32,fold,0)
            m2,m1=masks(32)
            def swap(x,y,sh,mask):
                return jnp.where(mask,x,pltpu.roll(y,sh,1)), jnp.where(mask,pltpu.roll(x,128-sh,1),y)
            def fin(i,_):
                rows=pl.ds(pl.multiple_of(i*32,32),32)
                for hh in range(2):
                    v=[N[pl.ds(i*256+4*hh+w,32,stride=8),:] for w in range(4)]
                    v[0],v[2]=swap(v[0],v[2],64,m2); v[1],v[3]=swap(v[1],v[3],64,m2)
                    v[0],v[1]=swap(v[0],v[1],32,m1); v[2],v[3]=swap(v[2],v[3],32,m1)
                    for q in range(4):
                        c=2*q+hh
                        out[rows,c*128:(c+1)*128]=v[q]
                return 0
            lax.fori_loop(0,TPD//32,fin,0,unroll=2)
    return pl.pallas_call(kernel,
        out_shape=jax.ShapeDtypeStruct((TPD,1024),jnp.float32),
        grid_spec=pltpu.PrefetchScalarGridSpec(num_scalar_prefetch=4,grid=(H,),
            in_specs=[pl.BlockSpec((512,32,128),lambda h,*_:(h,0,0)),
                      pl.BlockSpec((256,32,128),lambda h,*_:(h,0,0))],
            out_specs=pl.BlockSpec((TPD,1024),lambda h,*_:(0,0)),
            scratch_shapes=[pltpu.VMEM((ROWS*32,128),jnp.float32)]*4+[pltpu.VMEM((UG,32,128),jnp.float32),pltpu.VMEM((TPD*8,128),jnp.float32)]),
        compiler_params=pltpu.CompilerParams(vmem_limit_bytes=62*2**20,dimension_semantics=("arbitrary",),flags=flags or {}))

def pack_kernel(x, o, xf, of):
    lgq = lax.broadcasted_iota(jnp.int32, (128, 128), 1) // 32
    n2 = lgq < 2
    n1 = (lgq % 2) == 0

    def swap(x, y, sh, mask):
        return jnp.where(mask, x, pltpu.roll(y, sh, 1)), jnp.where(mask, pltpu.roll(x, 128 - sh, 1), y)

    for c in range(8):
        xf[...] = x[:, c * 128:(c + 1) * 128].astype(jnp.float32)
        v = [xf[pl.ds(q, 128, stride=4), :] for q in range(4)]
        v[0], v[2] = swap(v[0], v[2], 64, n2)
        v[1], v[3] = swap(v[1], v[3], 64, n2)
        v[0], v[1] = swap(v[0], v[1], 32, n1)
        v[2], v[3] = swap(v[2], v[3], 32, n1)
        for w in range(4):
            of[pl.ds(4 * c + w, 128, stride=32), :] = v[w]

    def cast(i, _):
        rows = pl.ds(pl.multiple_of(i * 512, 512), 512)
        o[rows, :] = of[rows, :].astype(jnp.bfloat16)
        return 0

    lax.fori_loop(0, 8, cast, 0)


def pack_tiles(x):
    return pl.pallas_call(
        pack_kernel,
        out_shape=jax.ShapeDtypeStruct((4096, 128), jnp.bfloat16),
        in_specs=[pl.BlockSpec(memory_space=pltpu.VMEM)],
        out_specs=pl.BlockSpec(memory_space=pltpu.VMEM),
        scratch_shapes=[pltpu.VMEM((512, 128), jnp.float32), pltpu.VMEM((4096, 128), jnp.float32)],
    )(x).reshape(128, 32, 128)

LISTS = 4
SROWS = 88


def sort_stage_a(stk, m_s, cum_s, pos_s, val_s, st_o):
    a, b, t = stk[0], stk[1], stk[2]
    g = lax.broadcasted_iota(jnp.int32, (16, STK), 0)
    cls = jnp.where(t < TPD, ((b - a) & 3) * 4 + (a & 3), 16)
    ic = lax.broadcasted_iota(jnp.int32, (16, STK), 0)
    fields = (a >> 2, b >> 2, (t & 511) >> 1, (t & 1) + 2 * (g & 7))
    for k in range(16):
        m_s[16 * k:16 * k + 16, :] = (ic == cls[k:k + 1, :]).astype(jnp.float32).astype(jnp.bfloat16)
        v = jnp.zeros((16, STK), jnp.float32)
        for n, f in enumerate(fields):
            v = jnp.where(ic == n, f[k:k + 1, :].astype(jnp.float32), v)
        val_s[16 * k:16 * k + 16, :] = v.astype(jnp.bfloat16)
    upper = (lax.broadcasted_iota(jnp.int32, (STK, STK), 0) <= lax.broadcasted_iota(jnp.int32, (STK, STK), 1))
    cum_s[...] = jnp.dot(m_s[...], upper.astype(jnp.float32).astype(jnp.bfloat16), preferred_element_type=jnp.float32)
    ic1 = lax.broadcasted_iota(jnp.int32, (16, 128), 0)
    for q in range(LISTS):
        tots = [jnp.broadcast_to(cum_s[16 * (4 * q + k):16 * (4 * q + k) + 16, STK - 1:STK], (16, 128)) for k in range(4)]
        total = tots[0] + tots[1] + tots[2] + tots[3]
        start = jnp.zeros((16, 128), jnp.float32)
        for c in range(15):
            start = start + jnp.where(ic1 > c, jnp.broadcast_to(total[c:c + 1, :], (16, 128)), 0.0)
        st_o[q, 0:16, :] = start.astype(jnp.int32)
        live = jnp.broadcast_to(start[15:16, :] + total[15:16, :], (8, 128))
        st_o[q, 16:24, :] = live.astype(jnp.int32)
        base = start
        for k in range(4):
            r = 16 * (4 * q + k)
            w = m_s[r:r + 16, :].astype(jnp.float32) * (cum_s[r:r + 16, :] + base[:, 0:1])
            pos_s[4 * q + k:4 * q + k + 1, :] = jnp.sum(w, axis=0, keepdims=True)
            base = base + tots[k]


def sort_stage_b(k, pos_s, val_s, acc_s):
    q = k // 4
    pos = pos_s[k:k + 1, :].astype(jnp.int32)
    v = val_s[16 * k:16 * k + 16, :]

    def part(i, _):
        rows = lax.broadcasted_iota(jnp.int32, (256, STK), 0) + (i * 256 + 1)
        pick = (rows == pos).astype(jnp.float32).astype(jnp.bfloat16)
        o = lax.dot_general(v, pick, (((1,), (1,)), ((), ())), preferred_element_type=jnp.float32)
        cols = pl.ds(pl.multiple_of(i * 256, 256), 256)
        if k % 4 == 0:
            acc_s[q, :, cols] = o
        else:
            acc_s[q, :, cols] = acc_s[q, :, cols] + o
        return 0

    lax.fori_loop(0, 4 * STK // 256, part, 0)


def sort_stage_c(acc_s, ia, ib, it):
    for q in range(LISTS):
        f = [acc_s[q, n:n + 1, :].astype(jnp.int32) for n in range(4)]
        gg = f[3] >> 1
        av = (gg & 3) * 128 + f[0]
        bv = ((gg >> 1) & 1) * 128 + f[1]
        tv = (f[2] * 2 + (f[3] & 1)) * 32
        for k in range(16):
            sl = slice(128 * k, 128 * k + 128)
            ia[16 * q + k:16 * q + k + 1, :] = av[:, sl]
            ib[16 * q + k:16 * q + k + 1, :] = bv[:, sl]
            it[16 * q + k:16 * q + k + 1, :] = tv[:, sl]
    z = jnp.zeros((SROWS - 64, 128), jnp.int32)
    ia[64:SROWS, :] = z
    ib[64:SROWS, :] = z
    it[64:SROWS, :] = z


SORT_OUT = [jax.ShapeDtypeStruct((SROWS, 128), jnp.int32)] * 3 + [jax.ShapeDtypeStruct((LISTS, 24, 128), jnp.int32)]
SORT_SCRATCH = [pltpu.VMEM((256, STK), jnp.bfloat16), pltpu.VMEM((256, STK), jnp.float32), pltpu.VMEM((16, STK), jnp.float32),
                pltpu.VMEM((256, STK), jnp.bfloat16), pltpu.VMEM((LISTS, 16, 4 * STK), jnp.float32)]
NC = 4


def gather_kernel(own, stk, left, right, relay, ia, ib, it, st_o, local_sem, send, recv, m_s, cum_s, pos_s, val_s, acc_s):
    r = lax.axis_index("row"); c = lax.axis_index("col")
    xl = lax.rem(c // 2, 2); k = lax.rem(c, 2); xh = lax.rem(r, 2)
    yp, ym = lax.rem(c + 4, 16), lax.rem(c + 12, 16)
    cx, ck = c + 2 - 4 * xl, c + 1 - 2 * k
    cxp, cxm = lax.rem(cx + 4, 16), lax.rem(cx + 12, 16)
    zp, zm = lax.rem(r + 2, 8), lax.rem(r + 6, 8)
    rx = r + 1 - 2 * xh
    rxp, rxm = lax.rem(rx + 2, 8), lax.rem(rx + 6, 8)
    y2, yx2 = lax.rem(c + 8, 16), lax.rem(cx + 8, 16)
    barrier = pltpu.get_barrier_semaphore()
    for d in ((r, yp), (r, ym), (r, cx), (r, ck), (zp, c), (zm, c), (rx, cx)):
        pl.semaphore_signal(barrier, inc=1, device_id=d, device_id_type=pl.DeviceIdType.MESH)
    pl.semaphore_wait(barrier, 7)
    copies = {}
    rows = own.shape[0] // NC

    def go(name, src, dst, device, j):
        n = len(copies)
        piece = pl.ds(j * rows, rows)
        cp = pltpu.make_async_remote_copy(src_ref=src.at[piece], dst_ref=dst.at[piece], send_sem=send.at[n],
                                          recv_sem=recv.at[n], device_id=device, device_id_type=pl.DeviceIdType.MESH)
        cp.start()
        copies[name, j] = cp

    def lf(name, i, device, j):
        go(name, left.at[i], left.at[i], device, j)

    def rt(name, i, device, j):
        go(name, right.at[i], right.at[i], device, j)

    def got(name, j):
        copies[name, j].wait_recv()

    r2, rx2 = lax.rem(r + 4, 8), lax.rem(rx + 4, 8)

    def raw(name, src, dst, device, j):
        n = len(copies)
        cp = pltpu.make_async_remote_copy(src_ref=src, dst_ref=dst, send_sem=send.at[n], recv_sem=recv.at[n],
                                          device_id=device, device_id_type=pl.DeviceIdType.MESH)
        cp.start()
        copies[name, j] = cp

    def piece(j):
        return pl.ds(j * rows, rows)

    for j in range(NC):
        go("a0", own, left.at[c], (r, cx), j)
        go("a1", own, left.at[c], (r, yp), j)
        go("a2", own, left.at[c], (r, ym), j)
        go("b1", own, right.at[r], (zp, c), j)
        go("b2", own, right.at[r], (zm, c), j)
    for j in range(NC):
        go("f0", own, left.at[c], (r, ck), j)
    l0 = pltpu.make_async_copy(own, left.at[c], local_sem.at[0])
    l1 = pltpu.make_async_copy(own, right.at[r], local_sem.at[1])
    l0.start()
    l1.start()
    sort_stage_a(stk, m_s, cum_s, pos_s, val_s, st_o)
    for j in range(NC):
        got("a0", j)
        go("b0", left.at[cx], right.at[r], (rx, cx), j)
        lf("f1", cx, (r, ck), j)
        got("a1", j)
        got("a2", j)
        if j < 2:
            lf("a5", ym, (r, yp), j)
        else:
            lf("a5", yp, (r, ym), j)
        lf("a3", cx, (r, yp), j)
        lf("a4", cx, (r, ym), j)
        lf("f2", ym, (r, ck), j)
        lf("f3", yp, (r, ck), j)
        got("b1", j)
        got("b2", j)
        if j < 3:
            rt("b5", zm, (zp, c), j)
        else:
            rt("b5", zp, (zm, c), j)
        sort_stage_b(j, pos_s, val_s, acc_s)
    for j in range(NC):
        got("b0", j)
        rt("b3", rx, (zp, c), j)
        rt("b4", rx, (zm, c), j)
        sort_stage_b(4 + j, pos_s, val_s, acc_s)
    got("b5", 0)
    raw("r", right.at[r2].at[piece(0)], relay.at[0], (r, cx), 0)
    got("b5", 1)
    raw("r", right.at[r2].at[piece(1)], relay.at[1], (rx, cx), 1)
    for j in range(NC):
        got("a5", j)
        lf("a6", y2, (r, cx), j)
        lf("f6", y2, (r, ck), j)
        if j == 1:
            got("r", 0)
            raw("b6", relay.at[0], right.at[r2].at[piece(0)], (rx, cx), 0)
            got("r", 1)
            raw("b6", relay.at[1], right.at[rx2].at[piece(1)], (r, cx), 1)
        got("a4", j)
        lf("f4", cxp, (r, ck), j)
        if j >= 2:
            got("b4", j)
            rt("b6", rxp, (zm, c), j)
        got("a3", j)
        lf("f5", cxm, (r, ck), j)
        sort_stage_b(8 + 2 * j, pos_s, val_s, acc_s)
        sort_stage_b(9 + 2 * j, pos_s, val_s, acc_s)
    for j in range(NC):
        got("a6", j)
        lf("f7", yx2, (r, ck), j)
    sort_stage_c(acc_s, ia, ib, it)
    got("b4", 0)
    got("b4", 1)
    got("b5", 2)
    got("b5", 3)
    for j in range(NC):
        for name in ("b3", "b6", "f0", "f1", "f2", "f3", "f4", "f5", "f6", "f7"):
            got(name, j)
    for cp in copies.values():
        cp.wait_send()
    l0.wait()
    l1.wait()


def gather(own, stk):
    shape = own.shape
    n = 90
    return pl.pallas_call(
        gather_kernel,
        out_shape=(jax.ShapeDtypeStruct((16,) + shape, own.dtype), jax.ShapeDtypeStruct((8,) + shape, own.dtype),
                   jax.ShapeDtypeStruct((2, shape[0] // NC) + shape[1:], own.dtype), *SORT_OUT),
        in_specs=[pl.BlockSpec(memory_space=pltpu.VMEM)] * 2,
        out_specs=(pl.BlockSpec(memory_space=pl.ANY),) * 3 + (pl.BlockSpec(memory_space=pltpu.VMEM),) * 4,
        scratch_shapes=[pltpu.SemaphoreType.DMA((2,)), pltpu.SemaphoreType.DMA((n,)), pltpu.SemaphoreType.DMA((n,))] + SORT_SCRATCH,
        compiler_params=pltpu.CompilerParams(collective_id=0, has_side_effects=True),
    )(own, stk)


def local(panels, stacks):
    left, right, _, ia, ib, it, starts = gather(pack_tiles(panels[0, 0]), stacks[:, 0, 0])
    out = make(4, 24)(ia.reshape(-1), ib.reshape(-1), it.reshape(-1), starts.reshape(-1, 128),
                      left.reshape(2048, 32, 128), right.reshape(1024, 32, 128))
    return out.reshape(1, 1, TPD, 1024)


def solution(mesh):
    in_specs = (P_("row", "col", None, None), P_(None, "row", "col", None, None))
    out_specs = P_("row", "col", None, None)
    return jax.shard_map(local, mesh=mesh, in_specs=in_specs, out_specs=out_specs, check_vma=False)
```

```python
import functools
import jax
import jax.numpy as jnp
from jax import lax
from jax.experimental import pallas as pl
from jax.sharding import PartitionSpec as P_
from jax.experimental.pallas import tpu as pltpu
TPD=512; STK=512
ROWS=520
def make(H=4, UG=16, flags=None):
    def kernel(a_s,b_s,t_s,st,L,R,out,C0,C1,C2,C3,P,N):
        C=[C0,C1,C2,C3]
        h=pl.program_id(0)
        lg=lax.broadcasted_iota(jnp.int32,(32,128),1)//32
        keep=[lg==s for s in range(4)]
        lt2=lg<2
        zero=jnp.zeros((32,128),jnp.bfloat16)
        @pl.when(h==0)
        def _():
            P[...]=jnp.zeros(P.shape,jnp.float32)
            def z(i,_):
                for s in range(4):
                    C[s][pl.ds(pl.multiple_of(i*64,64),64),:]=jnp.zeros((64,128),jnp.float32)
                return 0
            lax.fori_loop(0,ROWS//2,z,0,unroll=4)
        for d in range(4):
            s_=[st[h*24+d*4+p,0] for p in range(4)]
            e_=[st[h*24+d*4+p+1,0] for p in range(4)]
            n=functools.reduce(jnp.maximum,[e-s for s,e in zip(s_,e_)])
            nb=(n+UG-1)//UG
            off=h*2048
            def compute(i,s_=s_,d=d,off=off):
                base=[s+off+i*UG for s in s_]
                for u in range(0,UG,2):
                    ls=[];rs=[]
                    for k in range(2):
                        av=[];bv=[]
                        for p in range(4):
                            ix=base[p]+(u+k)
                            av.append(L[a_s[ix]]); bv.append(R[b_s[ix]])
                        ls.append(jnp.where(lt2,jnp.where(keep[0],av[0],av[1]),jnp.where(keep[2],av[2],av[3])))
                        rs.append(jnp.concatenate([jnp.where(keep[(p+d)%4],bv[p],zero) for p in range(4)],axis=0))
                    o=jnp.dot(jnp.concatenate(ls,axis=0),jnp.concatenate(rs,axis=1),preferred_element_type=jnp.float32)
                    P[u]=o[:32,:128]; P[u+1]=o[32:,128:]
            def scatter(i,check,s_=s_,e_=e_,d=d,off=off):
                base=[s+off+i*UG for s in s_]
                end=[e+off for e in e_]
                for u in range(UG):
                    v=P[u]
                    for p in range(4):
                        ix=base[p]+u
                        t=t_s[ix]
                        if check: t=jnp.where(ix<end[p],t,TPD*32)
                        c=C[(p+d)%4]
                        w_=pl.ds(pl.multiple_of(t,32),32)
                        c[w_,:]=c[w_,:]+v
            def step(i,_):
                scatter(i-1,True); compute(i)
                return 0
            @pl.when(n>0)
            def _():
                compute(0)
                lax.fori_loop(1,nb,step,0)
                scatter(nb-1,True)
        @pl.when(h==H-1)
        def _():
            def masks(rows):
                g_=lax.broadcasted_iota(jnp.int32,(rows,128),1)//32
                return g_<2,(g_%2)==0
            n2,n1=masks(8)
            g8=lax.broadcasted_iota(jnp.int32,(8,128),1)//32
            sel=[(g8==0)|(g8==3),n2]
            def fold(i,_):
                for w in range(32):
                    t=i*32+w
                    row=pl.multiple_of(t*32,32)
                    v=[]
                    for q in range(4):
                        x=[C[s][pl.ds(row+8*q,8),:] for s in range(4)]
                        v.append(jnp.where(n2,jnp.where(n1,x[0],x[1]),jnp.where(n1,x[2],x[3])))
                    z=[jnp.where(sel[k],v[k],v[k+2])+pltpu.roll(jnp.where(sel[k],v[k+2],v[k]),64,1) for k in range(2)]
                    N[pl.ds(pl.multiple_of(t*8,8),8),:]=jnp.where(n1,z[0],z[1])+pltpu.roll(jnp.where(n1,z[1],z[0]),32,1)
                return 0
            lax.fori_loop(0,TPD//32,fold,0)
            m2,m1=masks(32)
            def swap(x,y,sh,mask):
                return jnp.where(mask,x,pltpu.roll(y,sh,1)), jnp.where(mask,pltpu.roll(x,128-sh,1),y)
            def fin(i,_):
                rows=pl.ds(pl.multiple_of(i*32,32),32)
                for hh in range(2):
                    v=[N[pl.ds(i*256+4*hh+w,32,stride=8),:] for w in range(4)]
                    v[0],v[2]=swap(v[0],v[2],64,m2); v[1],v[3]=swap(v[1],v[3],64,m2)
                    v[0],v[1]=swap(v[0],v[1],32,m1); v[2],v[3]=swap(v[2],v[3],32,m1)
                    for q in range(4):
                        c=2*q+hh
                        out[rows,c*128:(c+1)*128]=v[q]
                return 0
            lax.fori_loop(0,TPD//32,fin,0,unroll=2)
    return pl.pallas_call(kernel,
        out_shape=jax.ShapeDtypeStruct((TPD,1024),jnp.float32),
        grid_spec=pltpu.PrefetchScalarGridSpec(num_scalar_prefetch=4,grid=(H,),
            in_specs=[pl.BlockSpec((512,32,128),lambda h,*_:(h,0,0)),
                      pl.BlockSpec((256,32,128),lambda h,*_:(h,0,0))],
            out_specs=pl.BlockSpec((TPD,1024),lambda h,*_:(0,0)),
            scratch_shapes=[pltpu.VMEM((ROWS*32,128),jnp.float32)]*4+[pltpu.VMEM((UG,32,128),jnp.float32),pltpu.VMEM((TPD*8,128),jnp.float32)]),
        compiler_params=pltpu.CompilerParams(vmem_limit_bytes=62*2**20,dimension_semantics=("arbitrary",),flags=flags or {}))

def pack_kernel(x, o, xf, of):
    lgq = lax.broadcasted_iota(jnp.int32, (128, 128), 1) // 32
    n2 = lgq < 2
    n1 = (lgq % 2) == 0

    def swap(x, y, sh, mask):
        return jnp.where(mask, x, pltpu.roll(y, sh, 1)), jnp.where(mask, pltpu.roll(x, 128 - sh, 1), y)

    for c in range(8):
        xf[...] = x[:, c * 128:(c + 1) * 128].astype(jnp.float32)
        v = [xf[pl.ds(q, 128, stride=4), :] for q in range(4)]
        v[0], v[2] = swap(v[0], v[2], 64, n2)
        v[1], v[3] = swap(v[1], v[3], 64, n2)
        v[0], v[1] = swap(v[0], v[1], 32, n1)
        v[2], v[3] = swap(v[2], v[3], 32, n1)
        for w in range(4):
            of[pl.ds(4 * c + w, 128, stride=32), :] = v[w]

    def cast(i, _):
        rows = pl.ds(pl.multiple_of(i * 512, 512), 512)
        o[rows, :] = of[rows, :].astype(jnp.bfloat16)
        return 0

    lax.fori_loop(0, 8, cast, 0)


def pack_tiles(x):
    return pl.pallas_call(
        pack_kernel,
        out_shape=jax.ShapeDtypeStruct((4096, 128), jnp.bfloat16),
        in_specs=[pl.BlockSpec(memory_space=pltpu.VMEM)],
        out_specs=pl.BlockSpec(memory_space=pltpu.VMEM),
        scratch_shapes=[pltpu.VMEM((512, 128), jnp.float32), pltpu.VMEM((4096, 128), jnp.float32)],
    )(x).reshape(128, 32, 128)

LISTS = 4
SROWS = 88


def sort_stage_a(stk, m_s, cum_s, pos_s, val_s, st_o):
    a, b, t = stk[0], stk[1], stk[2]
    g = lax.broadcasted_iota(jnp.int32, (16, STK), 0)
    cls = jnp.where(t < TPD, ((b - a) & 3) * 4 + (a & 3), 16)
    ic = lax.broadcasted_iota(jnp.int32, (16, STK), 0)
    fields = (a >> 2, b >> 2, (t & 511) >> 1, (t & 1) + 2 * (g & 7))
    for k in range(16):
        m_s[16 * k:16 * k + 16, :] = (ic == cls[k:k + 1, :]).astype(jnp.float32).astype(jnp.bfloat16)
        v = jnp.zeros((16, STK), jnp.float32)
        for n, f in enumerate(fields):
            v = jnp.where(ic == n, f[k:k + 1, :].astype(jnp.float32), v)
        val_s[16 * k:16 * k + 16, :] = v.astype(jnp.bfloat16)
    upper = (lax.broadcasted_iota(jnp.int32, (STK, STK), 0) <= lax.broadcasted_iota(jnp.int32, (STK, STK), 1))
    cum_s[...] = jnp.dot(m_s[...], upper.astype(jnp.float32).astype(jnp.bfloat16), preferred_element_type=jnp.float32)
    ic1 = lax.broadcasted_iota(jnp.int32, (16, 128), 0)
    for q in range(LISTS):
        tots = [jnp.broadcast_to(cum_s[16 * (4 * q + k):16 * (4 * q + k) + 16, STK - 1:STK], (16, 128)) for k in range(4)]
        total = tots[0] + tots[1] + tots[2] + tots[3]
        start = jnp.zeros((16, 128), jnp.float32)
        for c in range(15):
            start = start + jnp.where(ic1 > c, jnp.broadcast_to(total[c:c + 1, :], (16, 128)), 0.0)
        st_o[q, 0:16, :] = start.astype(jnp.int32)
        live = jnp.broadcast_to(start[15:16, :] + total[15:16, :], (8, 128))
        st_o[q, 16:24, :] = live.astype(jnp.int32)
        base = start
        for k in range(4):
            r = 16 * (4 * q + k)
            w = m_s[r:r + 16, :].astype(jnp.float32) * (cum_s[r:r + 16, :] + base[:, 0:1])
            pos_s[4 * q + k:4 * q + k + 1, :] = jnp.sum(w, axis=0, keepdims=True)
            base = base + tots[k]


def sort_stage_b(k, pos_s, val_s, acc_s):
    q = k // 4
    pos = pos_s[k:k + 1, :].astype(jnp.int32)
    v = val_s[16 * k:16 * k + 16, :]

    def part(i, _):
        rows = lax.broadcasted_iota(jnp.int32, (256, STK), 0) + (i * 256 + 1)
        pick = (rows == pos).astype(jnp.float32).astype(jnp.bfloat16)
        o = lax.dot_general(v, pick, (((1,), (1,)), ((), ())), preferred_element_type=jnp.float32)
        cols = pl.ds(pl.multiple_of(i * 256, 256), 256)
        if k % 4 == 0:
            acc_s[q, :, cols] = o
        else:
            acc_s[q, :, cols] = acc_s[q, :, cols] + o
        return 0

    lax.fori_loop(0, 4 * STK // 256, part, 0)


def sort_stage_c(acc_s, ia, ib, it):
    for q in range(LISTS):
        f = [acc_s[q, n:n + 1, :].astype(jnp.int32) for n in range(4)]
        gg = f[3] >> 1
        av = (gg & 3) * 128 + f[0]
        bv = ((gg >> 1) & 1) * 128 + f[1]
        tv = (f[2] * 2 + (f[3] & 1)) * 32
        for k in range(16):
            sl = slice(128 * k, 128 * k + 128)
            ia[16 * q + k:16 * q + k + 1, :] = av[:, sl]
            ib[16 * q + k:16 * q + k + 1, :] = bv[:, sl]
            it[16 * q + k:16 * q + k + 1, :] = tv[:, sl]
    z = jnp.zeros((SROWS - 64, 128), jnp.int32)
    ia[64:SROWS, :] = z
    ib[64:SROWS, :] = z
    it[64:SROWS, :] = z


SORT_OUT = [jax.ShapeDtypeStruct((SROWS, 128), jnp.int32)] * 3 + [jax.ShapeDtypeStruct((LISTS, 24, 128), jnp.int32)]
SORT_SCRATCH = [pltpu.VMEM((256, STK), jnp.bfloat16), pltpu.VMEM((256, STK), jnp.float32), pltpu.VMEM((16, STK), jnp.float32),
                pltpu.VMEM((256, STK), jnp.bfloat16), pltpu.VMEM((LISTS, 16, 4 * STK), jnp.float32)]
NC = 4


def gather_kernel(own, stk, left, right, relay, ia, ib, it, st_o, local_sem, send, recv, m_s, cum_s, pos_s, val_s, acc_s):
    r = lax.axis_index("row"); c = lax.axis_index("col")
    xl = lax.rem(c // 2, 2); k = lax.rem(c, 2); xh = lax.rem(r, 2)
    yp, ym = lax.rem(c + 4, 16), lax.rem(c + 12, 16)
    cx, ck = c + 2 - 4 * xl, c + 1 - 2 * k
    cxp, cxm = lax.rem(cx + 4, 16), lax.rem(cx + 12, 16)
    zp, zm = lax.rem(r + 2, 8), lax.rem(r + 6, 8)
    rx = r + 1 - 2 * xh
    rxp, rxm = lax.rem(rx + 2, 8), lax.rem(rx + 6, 8)
    y2, yx2 = lax.rem(c + 8, 16), lax.rem(cx + 8, 16)
    barrier = pltpu.get_barrier_semaphore()
    for d in ((r, yp), (r, ym), (r, cx), (r, ck), (zp, c), (zm, c), (rx, cx)):
        pl.semaphore_signal(barrier, inc=1, device_id=d, device_id_type=pl.DeviceIdType.MESH)
    pl.semaphore_wait(barrier, 7)
    copies = {}
    rows = own.shape[0] // NC

    def go(name, src, dst, device, j):
        n = len(copies)
        piece = pl.ds(j * rows, rows)
        cp = pltpu.make_async_remote_copy(src_ref=src.at[piece], dst_ref=dst.at[piece], send_sem=send.at[n],
                                          recv_sem=recv.at[n], device_id=device, device_id_type=pl.DeviceIdType.MESH)
        cp.start()
        copies[name, j] = cp

    def lf(name, i, device, j):
        go(name, left.at[i], left.at[i], device, j)

    def rt(name, i, device, j):
        go(name, right.at[i], right.at[i], device, j)

    def got(name, j):
        copies[name, j].wait_recv()

    r2, rx2 = lax.rem(r + 4, 8), lax.rem(rx + 4, 8)

    def raw(name, src, dst, device, j):
        n = len(copies)
        cp = pltpu.make_async_remote_copy(src_ref=src, dst_ref=dst, send_sem=send.at[n], recv_sem=recv.at[n],
                                          device_id=device, device_id_type=pl.DeviceIdType.MESH)
        cp.start()
        copies[name, j] = cp

    def piece(j):
        return pl.ds(j * rows, rows)

    for j in range(NC):
        go("a0", own, left.at[c], (r, cx), j)
        go("a1", own, left.at[c], (r, yp), j)
        go("a2", own, left.at[c], (r, ym), j)
        go("b1", own, right.at[r], (zp, c), j)
        go("b2", own, right.at[r], (zm, c), j)
    for j in range(NC):
        go("f0", own, left.at[c], (r, ck), j)
    l0 = pltpu.make_async_copy(own, left.at[c], local_sem.at[0])
    l1 = pltpu.make_async_copy(own, right.at[r], local_sem.at[1])
    l0.start()
    l1.start()
    sort_stage_a(stk, m_s, cum_s, pos_s, val_s, st_o)
    for j in range(NC):
        got("a0", j)
        go("b0", left.at[cx], right.at[r], (rx, cx), j)
        lf("f1", cx, (r, ck), j)
        got("a1", j)
        got("a2", j)
        if j < 2:
            lf("a5", ym, (r, yp), j)
        else:
            lf("a5", yp, (r, ym), j)
        lf("a3", cx, (r, yp), j)
        lf("a4", cx, (r, ym), j)
        lf("f2", ym, (r, ck), j)
        lf("f3", yp, (r, ck), j)
        got("b1", j)
        got("b2", j)
        if j < 3:
            rt("b5", zm, (zp, c), j)
        else:
            rt("b5", zp, (zm, c), j)
        sort_stage_b(j, pos_s, val_s, acc_s)
    for j in range(NC):
        got("b0", j)
        rt("b3", rx, (zp, c), j)
        rt("b4", rx, (zm, c), j)
    got("b5", 0)
    raw("r", right.at[r2].at[piece(0)], relay.at[0], (r, cx), 0)
    got("b5", 1)
    raw("r", right.at[r2].at[piece(1)], relay.at[1], (rx, cx), 1)
    for j in range(NC):
        got("a5", j)
        lf("a6", y2, (r, cx), j)
        lf("f6", y2, (r, ck), j)
        if j == 1:
            got("r", 0)
            raw("b6", relay.at[0], right.at[r2].at[piece(0)], (rx, cx), 0)
            got("r", 1)
            raw("b6", relay.at[1], right.at[rx2].at[piece(1)], (r, cx), 1)
        got("a4", j)
        lf("f4", cxp, (r, ck), j)
        if j >= 2:
            got("b4", j)
            rt("b6", rxp, (zm, c), j)
        got("a3", j)
        lf("f5", cxm, (r, ck), j)
        for k in range(3):
            sort_stage_b(4 + 3 * j + k, pos_s, val_s, acc_s)
    for j in range(NC):
        got("a6", j)
        lf("f7", yx2, (r, ck), j)
    sort_stage_c(acc_s, ia, ib, it)
    got("b4", 0)
    got("b4", 1)
    got("b5", 2)
    got("b5", 3)
    for j in range(NC):
        for name in ("b3", "b6", "f0", "f1", "f2", "f3", "f4", "f5", "f6", "f7"):
            got(name, j)
    for cp in copies.values():
        cp.wait_send()
    l0.wait()
    l1.wait()


def gather(own, stk):
    shape = own.shape
    n = 90
    return pl.pallas_call(
        gather_kernel,
        out_shape=(jax.ShapeDtypeStruct((16,) + shape, own.dtype), jax.ShapeDtypeStruct((8,) + shape, own.dtype),
                   jax.ShapeDtypeStruct((2, shape[0] // NC) + shape[1:], own.dtype), *SORT_OUT),
        in_specs=[pl.BlockSpec(memory_space=pltpu.VMEM)] * 2,
        out_specs=(pl.BlockSpec(memory_space=pl.ANY),) * 3 + (pl.BlockSpec(memory_space=pltpu.VMEM),) * 4,
        scratch_shapes=[pltpu.SemaphoreType.DMA((2,)), pltpu.SemaphoreType.DMA((n,)), pltpu.SemaphoreType.DMA((n,))] + SORT_SCRATCH,
        compiler_params=pltpu.CompilerParams(collective_id=0, has_side_effects=True),
    )(own, stk)


def local(panels, stacks):
    left, right, _, ia, ib, it, starts = gather(pack_tiles(panels[0, 0]), stacks[:, 0, 0])
    out = make(4, 24)(ia.reshape(-1), ib.reshape(-1), it.reshape(-1), starts.reshape(-1, 128),
                      left.reshape(2048, 32, 128), right.reshape(1024, 32, 128))
    return out.reshape(1, 1, TPD, 1024)


def solution(mesh):
    in_specs = (P_("row", "col", None, None), P_(None, "row", "col", None, None))
    out_specs = P_("row", "col", None, None)
    return jax.shard_map(local, mesh=mesh, in_specs=in_specs, out_specs=out_specs, check_vma=False)
```
